128 devices in a mesh: row: 8 (over x, core), col: 16 (over y, z).
Axes of the slice: x: 4, y: 4, z: 4, core: 2. Of those that a mesh axis runs over, the one named last changes fastest.
Arguments:
- displacement: float32 [3, 64, 128, 8, 384], P(None, 'row', 'col'), may hold values from -6 to 6
- flux: float32 [16384, 384], P(('row', 'col')), may hold values from -6 to 6
- stiffness: float32 [64, 128, 8], P('row', 'col'), may hold values from 0.3 to 3
- mixing: float32 [3, 3], replicated, may hold values from -3.5 to 3.5
- single_layer: bfloat16 [16384, 16384], P('row', 'col'), may hold values from -0.09375 to 0.09375
- double_layer: bfloat16 [16384, 16384], P('row', 'col'), may hold values from -0.09375 to 0.09375
- near_blocks: bfloat16 [64, 16, 128, 128], P('row', 'col'), may hold values from -1 to 1
- near_rows: int32 [64, 16], P('row', 'col'), may hold values from 0 to 15
- near_cols: int32 [64, 16], P('row', 'col'), may hold values from 0 to 7
- near_counts: int32 [8, 16], P('row', 'col'), may hold values from 1 to 8, as said below
- routes: int32 [16384], P(('row', 'col')), may hold values from 0 to 127, as said below
Outputs:
- new_displacement: float32 [3, 64, 128, 8, 384], P(None, 'row', 'col')
- new_flux: float32 [16384, 384], P(('row', 'col'))
The draws below stay inside these ranges and needn't reach their ends.
Inputs may be any that keep to these rules, and one draw needn't show every extreme that they name: `routes`: each device's 128 values are a permutation of 0 to 127; value q sends the panel to tile column q // 8. `near_counts`: some tile has all 8 places live.
All inputs are finite; a program needn't handle non-finite values.
Results may differ from the reference program's by a relative error of at most 0.004.
Values may be sent and summed in bfloat16 or wider, within the bound.
No kernel may reach another device: no remote copies, remote signals or barrier semaphores. Data moves between devices by JAX's collectives and lax.ppermute only.
A program may use at most 128 MiB of HBM per device.

```python
import math
import jax
import jax.numpy as jnp
from jax import lax

CX = 8
CY = 8
CZ = 8
WAVES = 384
PB = 128
NEAR = 8
PO = 128
SLOTS = 8
NP = 16384
TR = 2048
TC = 1024
NX = 64
NY = 128
N_ROW = 8
N_COL = 16


def draw_routes(key, part):
    owners = NP // PO
    keys = jax.random.split(jax.random.fold_in(key, 11), owners)
    perms = jax.vmap(lambda one: jax.random.permutation(one, PO))(keys)
    return perms.reshape(NP).astype(jnp.int32)


def draw_near_counts(key, part):
    first = jax.random.fold_in(key, 21)
    second = jax.random.fold_in(key, 22)
    counts = jax.random.randint(first, (N_ROW * N_COL,), 1, NEAR + 1)
    where = jax.random.randint(second, (), 0, N_ROW * N_COL)
    counts = counts.at[where].set(NEAR)
    return counts.reshape(N_ROW, N_COL).astype(jnp.int32)


def touch_ends(array, stream_key, low, largest):
    index_at = [jax.random.randint(jax.random.fold_in(stream_key, axis), (), 0, length) for axis, length in enumerate(array.shape)]
    longest = array.shape.index(max(array.shape))
    neighbour = index_at[:longest] + [(index_at[longest] + 1) % array.shape[longest]] + index_at[longest + 1:]
    return array.at[tuple(index_at)].set(low).at[tuple(neighbour)].set(largest)


def level_of(own_key, extent, shards, smallest, largest):
    gain = 1.0
    for dim, blocks in shards:
        draws = jax.random.uniform(jax.random.fold_in(jax.random.fold_in(own_key, 6), dim), (blocks,), jnp.float32, smallest / len(shards), largest / len(shards))
        gain = gain * jnp.repeat(jnp.exp(draws), extent[dim] // blocks).reshape((-1,) + (1,) * (len(extent) - 1 - dim))
    return gain


def gaussian(key, extent, deviation, reach, cuts=(), kind=jnp.bfloat16):
    factor_of = level_of(key, extent, cuts, -0.22, 0.18) if cuts else 1.0
    array = jax.random.normal(key, extent, jnp.float32) * deviation * factor_of
    return jnp.minimum(jnp.maximum(array, -reach), reach).astype(kind)


def setup_inputs(seed: int = 0) -> dict:
    seeds = jax.random.split(jax.random.key(seed), 12)
    displacement = gaussian(seeds[0], (3, NX, NY, CZ, WAVES), 1.0, 6.0, ((1, 8), (2, 16)), jnp.float32)
    flux = gaussian(seeds[1], (NP, WAVES), 1.0, 6.0, ((0, 128),), jnp.float32)
    stiffness = jnp.clip(jnp.exp(math.log(3.0) - 2.3025851 * jax.random.uniform(seeds[2], (NX, NY, CZ), jnp.float32) ** level_of(seeds[2], (NX, NY, CZ), ((0, 8), (1, 16)), -0.2, 0.2)), 0.3, 3.0)
    mixing = gaussian(seeds[3], (3, 3), 3 ** -0.5, 3.5, (), jnp.float32)
    single_layer = gaussian(seeds[4], (NP, NP), (NP // 4) ** -0.5, 0.09375, ((0, 8), (1, 16)))
    double_layer = gaussian(seeds[5], (NP, NP), (NP // 4) ** -0.5, 0.09375, ((0, 8), (1, 16)))
    near_blocks = gaussian(seeds[6], (N_ROW * NEAR, N_COL, PB, PB), (PB // 4) ** -0.5, 1.0, ((0, 8), (1, 16)))
    near_rows = touch_ends(jax.random.randint(seeds[7], (N_ROW * NEAR, N_COL), 0, TR // PB), jax.random.fold_in(seeds[7], 1), 0, (TR // PB) - 1).astype(jnp.int32)
    near_cols = touch_ends(jax.random.randint(seeds[8], (N_ROW * NEAR, N_COL), 0, TC // PB), jax.random.fold_in(seeds[8], 1), 0, (TC // PB) - 1).astype(jnp.int32)
    near_counts = draw_near_counts(jax.random.fold_in(seeds[11], 71), 0)
    routes = draw_routes(jax.random.fold_in(seeds[11], 71), 0)
    return dict(displacement=displacement, flux=flux, stiffness=stiffness, mixing=mixing, single_layer=single_layer, double_layer=double_layer, near_blocks=near_blocks, near_rows=near_rows, near_cols=near_cols, near_counts=near_counts, routes=routes)


def apply_stiffness(field, stiffness, mixing):
    padded = jnp.pad(field, ((0, 0), (1, 1), (1, 1), (1, 1), (0, 0)))
    beside = padded[:, 2:, 1:-1, 1:-1] + padded[:, :-2, 1:-1, 1:-1]
    beside = beside + padded[:, 1:-1, 2:, 1:-1] + padded[:, 1:-1, :-2, 1:-1]
    beside = beside + padded[:, 1:-1, 1:-1, 2:] + padded[:, 1:-1, 1:-1, :-2]
    mixed = jnp.einsum("ij,jxyzq->ixyzq", mixing, field, precision=lax.Precision.HIGHEST)
    return stiffness[None, :, :, :, None] * (field - beside / 6.0) + mixed


def take_trace(field):
    faces = jnp.stack([field[2, :, :, 0], field[2, :, :, CZ - 1]], 0)
    faces = faces.reshape(2, N_ROW, CX, N_COL, CY, WAVES).transpose(1, 3, 0, 2, 4, 5)
    return faces.reshape(NP, WAVES)


def spread_trace(values):
    faces = values.reshape(N_ROW, N_COL, 2, CX, CY, WAVES).transpose(2, 0, 3, 1, 4, 5)
    return faces.reshape(2, NX, NY, WAVES)


def to_routed(values, routes):
    owners = N_ROW * N_COL
    table = routes.reshape(owners, PO)
    local = values.reshape(owners, PO, WAVES)
    packed = jnp.zeros_like(local).at[jnp.arange(owners)[:, None], table].set(local)
    packed = packed.reshape(owners, N_COL, SLOTS, WAVES).transpose(1, 0, 2, 3)
    return packed.reshape(NP, WAVES)


def apply_once(field, flux, stiffness, mixing, single_layer, double_layer, near_blocks, near_rows, near_cols, near_counts, routes):
    trace = take_trace(field)
    routed_phi = to_routed(flux.astype(jnp.bfloat16), routes)
    routed_w = to_routed(trace.astype(jnp.bfloat16), routes)

    def far_rows(index):
        start = index * TR
        left = lax.dynamic_slice_in_dim(single_layer, start, TR, 0)
        right = lax.dynamic_slice_in_dim(double_layer, start, TR, 0)
        return jnp.dot(left, routed_phi, preferred_element_type=jnp.float32) + jnp.dot(right, routed_w, preferred_element_type=jnp.float32)

    far = lax.map(far_rows, jnp.arange(N_ROW)).reshape(NP, WAVES)
    blocks = near_blocks.reshape(N_ROW, NEAR, N_COL, PB, PB).astype(jnp.float32)
    columns = routed_phi.reshape(N_COL, TC // PB, PB, WAVES)
    cols_index = near_cols.reshape(N_ROW, NEAR, N_COL)
    picked = columns[jnp.arange(N_COL)[None, None, :], cols_index].astype(jnp.float32)
    products = jnp.einsum("rkcab,rkcbq->rkcaq", blocks, picked, precision=lax.Precision.HIGHEST)
    live = (jnp.arange(NEAR)[None, :, None] < near_counts[:, None, :]).astype(jnp.float32)
    rows_index = near_rows.reshape(N_ROW, NEAR, N_COL)
    onehot = (rows_index[..., None] == jnp.arange(TR // PB)[None, None, None, :]).astype(jnp.float32) * live[..., None]
    near = jnp.einsum("rkci,rkcaq->riaq", onehot, products, precision=lax.Precision.HIGHEST).reshape(NP, WAVES)
    new_flux = far + near - 0.5 * trace
    spread = spread_trace(flux)
    new_field = apply_stiffness(field, stiffness, mixing)
    new_field = new_field.at[2, :, :, 0].add(-spread[0])
    new_field = new_field.at[2, :, :, CZ - 1].add(-spread[1])
    return new_field, new_flux


def reference(displacement, flux, stiffness, mixing, single_layer, double_layer, near_blocks, near_rows, near_cols, near_counts, routes):
    field, values = displacement, flux
    for step in range(2):
        field, values = apply_once(field, values, stiffness, mixing, single_layer, double_layer, near_blocks, near_rows, near_cols, near_counts, routes)
    return field, values
```

```python
import jax
import jax.numpy as jnp
from jax import lax
from jax.experimental import pallas as pl
from jax.experimental.pallas import tpu as pltpu
from jax.sharding import PartitionSpec as P

BF = jnp.bfloat16
F32 = jnp.float32
WAVES = 384
LANES = 128


def onehot(keys, count):
    rows = lax.broadcasted_iota(jnp.int32, (count, keys.shape[1]), 0)
    return (rows == keys).astype(F32).astype(BF)


def pack_kernel(flux_ref, comp_ref, route_ref, face_ref, out_ref):
    by_panel = onehot(route_ref[...], 128)
    by_cell = onehot(face_ref[...], 128)
    out_ref[:, 0:WAVES] = jnp.dot(by_panel, flux_ref[...].astype(BF), preferred_element_type=F32).astype(BF)
    cells = comp_ref[...].reshape(512, WAVES).astype(BF)
    out_ref[:, WAVES : 2 * WAVES] = jnp.dot(by_cell, cells, preferred_element_type=F32).astype(BF)
    out_ref[:, 2 * WAVES :] = jnp.broadcast_to(route_ref[...].astype(F32), (128, 128)).astype(BF)


def pack(flux, field, route_row, face_row):
    return pl.pallas_call(
        pack_kernel,
        grid=(1,),
        in_specs=[
            pl.BlockSpec((128, WAVES), lambda i: (0, 0)),
            pl.BlockSpec((None, 8, 8, 8, WAVES), lambda i: (2, 0, 0, 0, 0)),
            pl.BlockSpec((1, 128), lambda i: (0, 0)),
            pl.BlockSpec((1, 512), lambda i: (0, 0)),
        ],
        out_specs=pl.BlockSpec((128, 2 * WAVES + 128), lambda i: (0, 0)),
        out_shape=jax.ShapeDtypeStruct((128, 2 * WAVES + 128), BF),
        name="pack",
    )(flux, field, route_row, face_row)


def stencil_kernel(first, mix_ref, *refs):
    if first:
        u_ref, xl, xh, yl, yh, st_ref, flux_ref, route_ref, out_ref, w_ref, wp_ref, f0, f1, f2, f3 = refs
    else:
        u_ref, xl, xh, yl, yh, st_ref, out_ref = refs
    depth = lax.broadcasted_iota(jnp.int32, (8, LANES), 0)
    bottom = depth == 0
    top = depth == 7
    mix = [[mix_ref[i, j] for j in range(3)] for i in range(3)]

    def plane(x, below, above):
        for y in range(8):
            cell = [u_ref[c, x, y] for c in range(3)]
            stiff = jnp.broadcast_to(st_ref[x, y], (8, LANES))
            for c in range(3):
                u = cell[c]
                total = below(c, y) + above(c, y)
                total = total + (u_ref[c, x, y - 1] if y > 0 else yl[c, x].astype(F32))
                total = total + (u_ref[c, x, y + 1] if y < 7 else yh[c, x].astype(F32))
                total = total + jnp.where(bottom, 0.0, pltpu.roll(u, 1, 0))
                total = total + jnp.where(top, 0.0, pltpu.roll(u, 7, 0))
                mixed = mix[c][0] * cell[0] + mix[c][1] * cell[1] + mix[c][2] * cell[2]
                value = stiff * (u - total * (1.0 / 6.0)) + mixed
                if first and c == 2:
                    low = flux_ref[pl.ds(x * 8 + y, 1), :]
                    high = flux_ref[pl.ds(64 + x * 8 + y, 1), :]
                    value = value - jnp.where(bottom, low, jnp.where(top, high, 0.0))
                    w_ref[pl.ds(x * 8 + y, 1), :] = value[0:1]
                    w_ref[pl.ds(64 + x * 8 + y, 1), :] = value[7:8]
                out_ref[c, x, y] = value
                if first:
                    if y == 0:
                        f2[c, x] = value.astype(BF)
                    if y == 7:
                        f3[c, x] = value.astype(BF)

    plane(0, lambda c, y: xl[c, y].astype(F32), lambda c, y: u_ref[c, 1, y])

    def step(x, carry):
        plane(x, lambda c, y: u_ref[c, x - 1, y], lambda c, y: u_ref[c, x + 1, y])
        return carry

    lax.fori_loop(1, 7, step, 0)
    plane(7, lambda c, y: u_ref[c, 6, y], lambda c, y: xh[c, y].astype(F32))
    if first:
        f0[...] = out_ref[:, 0].astype(BF)
        f1[...] = out_ref[:, 7].astype(BF)
        wp_ref[...] = jnp.dot(onehot(route_ref[...], 128), w_ref[...].astype(BF), preferred_element_type=F32).astype(BF)


def stencil(field, halos, stiffness, mixing, flux=None, route_row=None):
    first = flux is not None
    whole = pl.BlockSpec((3, 8, 8, 8, LANES), lambda i: (0, 0, 0, 0, i))
    face = pl.BlockSpec((3, 8, 8, LANES), lambda i: (0, 0, 0, i))
    panel = pl.BlockSpec((128, LANES), lambda i: (0, i))
    in_specs = [pl.BlockSpec(memory_space=pltpu.SMEM), whole, face, face, face, face,
                pl.BlockSpec((8, 8, 8, 1), lambda i: (0, 0, 0, 0))]
    args = [mixing, field, *halos, stiffness]
    out_specs = [whole]
    out_shape = [jax.ShapeDtypeStruct(field.shape, F32)]
    if first:
        in_specs += [panel, pl.BlockSpec((1, 128), lambda i: (0, 0))]
        args += [flux, route_row]
        out_specs += [panel, panel, face, face, face, face]
        out_shape += [jax.ShapeDtypeStruct((128, WAVES), F32), jax.ShapeDtypeStruct((128, WAVES), BF)]
        out_shape += [jax.ShapeDtypeStruct((3, 8, 8, WAVES), BF)] * 4
    return pl.pallas_call(
        lambda *refs: stencil_kernel(first, *refs),
        grid=(WAVES // LANES,),
        in_specs=in_specs,
        out_specs=out_specs,
        out_shape=out_shape,
        name="stencil_first" if first else "stencil_second",
    )(*args)


def boundary_kernel(first, order_ref, rows_ref, cols_ref, count_ref, *refs):
    chunks = refs[:8]
    single_ref, double_ref, near_ref, extra_ref = refs[8:12]
    refs = refs[12:]
    if first:
        key_ref, out_ref, phi_ref, w_ref, acc_ref = refs
    else:
        out_ref, phi_ref, w_ref, acc_ref = refs
    i = pl.program_id(0)

    @pl.when(i == 0)
    def _():
        for k in range(8):
            at = pl.multiple_of(order_ref[k] * 128, 128)
            phi_ref[pl.ds(at, 128), :] = chunks[k][0]
            w_ref[pl.ds(at, 128), :] = chunks[k][1]

    acc_ref[...] = jnp.dot(single_ref[...], phi_ref[...], preferred_element_type=F32) + jnp.dot(
        double_ref[...], w_ref[...], preferred_element_type=F32
    )
    for k in range(8):
        @pl.when((k < count_ref[0]) & (rows_ref[k] // 2 == i))
        def _():
            row = pl.multiple_of((rows_ref[k] % 2) * 128, 128)
            col = pl.multiple_of(cols_ref[k] * 128, 128)
            acc_ref[pl.ds(row, 128), :] += jnp.dot(
                near_ref[k], phi_ref[pl.ds(col, 128), :], preferred_element_type=F32
            )
    total = acc_ref[...].astype(BF)
    if first:
        m = lax.broadcasted_iota(jnp.int32, (256, 256), 0)
        place = (m // 16) * 8 + m % 8 + 128 * ((m // 8) % 2)
        select = (place == key_ref[...]).astype(F32).astype(BF)
        packed = jnp.dot(select, total, preferred_element_type=F32).astype(BF)
        out_ref[:, pl.ds(pl.multiple_of(i * 16, 16), 16), :] = packed.reshape(16, 16, WAVES)

        @pl.when(i == 7)
        def _():
            out_ref[:, 128:136, :] = extra_ref[...]
    else:
        out_ref[:, 0:128, :] = total.reshape(2, 128, WAVES)
        out_ref[:, 128:136, :] = extra_ref[...]


def boundary(order, near, chunks, single_layer, double_layer, extra, keys=None):
    near_blocks, near_rows, near_cols, near_count = near
    first = keys is not None
    chunk = pl.BlockSpec((2, 128, WAVES), lambda i, *_: (0, 0, 0))
    tile = pl.BlockSpec((256, 1024), lambda i, *_: (i, 0))
    in_specs = [chunk] * 8 + [tile, tile, pl.BlockSpec((8, 128, 128), lambda i, *_: (0, 0, 0))]
    args = [*chunks, single_layer, double_layer, near_blocks, extra]
    if first:
        in_specs += [pl.BlockSpec((16, 8, WAVES), lambda i, *_: (0, 0, 0)),
                     pl.BlockSpec((None, 1, 256), lambda i, *_: (i, 0, 0))]
        args += [keys]
        out_spec = pl.BlockSpec((16, 136, WAVES), lambda i, *_: (0, 0, 0))
    else:
        in_specs += [pl.BlockSpec((2, 8, WAVES), lambda i, *_: (i, 0, 0))]
        out_spec = pl.BlockSpec((2, 136, WAVES), lambda i, *_: (i, 0, 0))
    return pl.pallas_call(
        lambda *refs: boundary_kernel(first, *refs),
        grid_spec=pltpu.PrefetchScalarGridSpec(
            num_scalar_prefetch=4,
            grid=(8,),
            in_specs=in_specs,
            out_specs=out_spec,
            scratch_shapes=[
                pltpu.VMEM((1024, WAVES), BF),
                pltpu.VMEM((1024, WAVES), BF),
                pltpu.VMEM((256, WAVES), F32),
            ],
        ),
        out_shape=jax.ShapeDtypeStruct((16, 136, WAVES), BF),
        name="boundary_first" if first else "boundary_second",
    )(order, near_rows, near_cols, near_count, *args)


def middle_kernel(got_ref, chunk_ref, out_ref):
    total = got_ref[0, 0:128].astype(F32)
    for k in range(1, 16):
        total = total + got_ref[k, 0:128].astype(F32)
    out_ref[0] = (total - 0.5 * chunk_ref[...].astype(F32)).astype(BF)
    out_ref[1] = got_ref[:, 128:136, :].reshape(128, LANES)


def middle(got, chunk):
    return pl.pallas_call(
        middle_kernel,
        grid=(WAVES // LANES,),
        in_specs=[
            pl.BlockSpec((16, 136, LANES), lambda i: (0, 0, i)),
            pl.BlockSpec((None, 128, LANES), lambda i: (1, 0, i)),
        ],
        out_specs=pl.BlockSpec((2, 128, LANES), lambda i: (0, 0, i)),
        out_shape=jax.ShapeDtypeStruct((2, 128, WAVES), BF),
        name="middle",
    )(got, chunk)


def last_kernel(got_ref, w_ref, route_ref, comp_ref, flux_ref, out_ref, mid_ref):
    total = got_ref[0, 0:128].astype(F32)
    for k in range(1, 16):
        total = total + got_ref[k, 0:128].astype(F32)
    flux_ref[...] = total - 0.5 * w_ref[...]
    picker = (lax.broadcasted_iota(jnp.int32, (128, 128), 1) == route_ref[...]).astype(F32).astype(BF)
    mid_ref[...] = jnp.dot(picker, got_ref[:, 128:136, :].reshape(128, LANES), preferred_element_type=F32)
    depth = lax.broadcasted_iota(jnp.int32, (8, LANES), 0)

    def step(x, carry):
        for y in range(8):
            low = mid_ref[pl.ds(x * 8 + y, 1), :]
            high = mid_ref[pl.ds(64 + x * 8 + y, 1), :]
            out_ref[x, y] = comp_ref[x, y] - jnp.where(depth == 0, low, jnp.where(depth == 7, high, 0.0))
        return carry

    lax.fori_loop(0, 8, step, 0)


def last(got, trace, route_column, field):
    comp = pl.BlockSpec((None, 8, 8, 8, LANES), lambda i: (2, 0, 0, 0, i))
    panel = pl.BlockSpec((128, LANES), lambda i: (0, i))
    return pl.pallas_call(
        last_kernel,
        grid=(WAVES // LANES,),
        in_specs=[
            pl.BlockSpec((16, 136, LANES), lambda i: (0, 0, i)),
            panel,
            pl.BlockSpec((128, 1), lambda i: (0, 0)),
            comp,
        ],
        out_specs=[panel, comp],
        out_shape=[jax.ShapeDtypeStruct((128, WAVES), F32), jax.ShapeDtypeStruct(field.shape, F32)],
        scratch_shapes=[pltpu.VMEM((128, LANES), F32)],
        input_output_aliases={3: 1},
        name="last",
    )(got, trace, route_column, field)


def shifted(count, by):
    return [(i, (i + by) % count) for i in range(count)]


def across_rows(chunk):
    row = lax.axis_index("row")
    mine = [chunk] + [lax.ppermute(chunk, "row", shifted(8, k)) for k in (4, 2, 6)]
    beside = [lax.ppermute(one, "row", [(i, i ^ 1) for i in range(8)]) for one in mine]
    order = [(row - k) % 8 for k in (0, 4, 2, 6)]
    order = jnp.stack(order + [one ^ 1 for one in order]).astype(jnp.int32)
    return mine + beside, order


def swap_faces(faces):
    low_x, high_x, low_y, high_y = faces
    up = lambda n: [(i, i + 1) for i in range(n - 1)]
    down = lambda n: [(i + 1, i) for i in range(n - 1)]
    return (
        lax.ppermute(high_x, "row", up(8)),
        lax.ppermute(low_x, "row", down(8)),
        lax.ppermute(high_y, "col", up(16)),
        lax.ppermute(low_y, "col", down(16)),
    )


def local(
    displacement,
    flux,
    stiffness,
    mixing,
    single_layer,
    double_layer,
    near_blocks,
    near_rows,
    near_cols,
    near_counts,
    routes,
):
    near = (near_blocks.reshape(8, 128, 128), near_rows.reshape(8), near_cols.reshape(8), near_counts.reshape(1))
    route_row = routes.reshape(1, 128)
    ends = routes.reshape(2, 64)
    face_row = jnp.concatenate(
        [ends[0][:, None], jnp.full((64, 6), -1, jnp.int32), ends[1][:, None]], axis=1
    ).reshape(1, 512)

    packed = pack(flux, displacement, route_row, face_row)
    got = lax.all_to_all(packed.reshape(16, 8, 2 * WAVES + 128), "col", 0, 0, tiled=True)
    chunk = jnp.stack(
        [got[:, :, :WAVES].reshape(128, WAVES), got[:, :, WAVES : 2 * WAVES].reshape(128, WAVES)], 0
    )
    keys = got[:, 0, 2 * WAVES :].astype(jnp.int32).reshape(8, 2, 128)
    keys = (keys + jnp.array([0, 128], jnp.int32)[None, :, None]).reshape(8, 1, 256)

    faces = [
        displacement[:, 0].astype(BF),
        displacement[:, 7].astype(BF),
        displacement[:, :, 0].astype(BF),
        displacement[:, :, 7].astype(BF),
    ]
    stiff = stiffness[..., None]
    field, trace, outgoing, *faces = stencil(displacement, swap_faces(faces), stiff, mixing, flux, route_row)

    chunks, order = across_rows(chunk)
    sums = boundary(order, near, chunks, single_layer, double_layer, outgoing.reshape(16, 8, WAVES), keys)
    got = lax.all_to_all(sums, "col", 0, 0, tiled=True)
    (field,) = stencil(field, swap_faces(faces), stiff, mixing)
    chunk = middle(got, chunk)

    chunks, order = across_rows(chunk)
    sums = boundary(order, near, chunks, single_layer, double_layer, chunk[0].reshape(16, 8, WAVES))
    got = lax.all_to_all(sums, "col", 0, 0, tiled=True)
    new_flux, field = last(got, trace, routes.reshape(128, 1), field)
    return (field, new_flux)


def solution(mesh):
    return jax.shard_map(
        local,
        mesh=mesh,
        in_specs=(
            P(None, "row", "col", None, None),
            P(("row", "col"), None),
            P("row", "col", None),
            P(),
            P("row", "col"),
            P("row", "col"),
            P("row", "col", None, None),
            P("row", "col"),
            P("row", "col"),
            P("row", "col"),
            P(("row", "col")),
        ),
        out_specs=(P(None, "row", "col", None, None), P(("row", "col"), None)),
        check_vma=False,
    )
```

```python
import jax
import jax.numpy as jnp
from jax import lax
from jax.experimental import pallas as pl
from jax.experimental.pallas import tpu as pltpu
from jax.sharding import PartitionSpec as P

BF = jnp.bfloat16
F32 = jnp.float32
WAVES = 384
LANES = 128
ROWS = 512
LIMIT = 24


def onehot(keys, count):
    rows = lax.broadcasted_iota(jnp.int32, (count, keys.shape[1]), 0)
    return (rows == keys).astype(F32).astype(BF)


def pack_kernel(flux_ref, comp_ref, route_ref, out_ref, trace_ref):
    by_panel = onehot(route_ref[...], 128)
    out_ref[:, 0:WAVES] = jnp.dot(by_panel, flux_ref[...].astype(BF), preferred_element_type=F32).astype(BF)

    def step(x, carry):
        for y in range(8):
            trace_ref[pl.ds(x * 8 + y, 1), :] = comp_ref[x, y, 0:1]
            trace_ref[pl.ds(64 + x * 8 + y, 1), :] = comp_ref[x, y, 7:8]
        return carry

    lax.fori_loop(0, 8, step, 0)
    out_ref[:, WAVES : 2 * WAVES] = jnp.dot(
        by_panel, trace_ref[...].astype(BF), preferred_element_type=F32
    ).astype(BF)
    out_ref[:, 2 * WAVES :] = jnp.broadcast_to(route_ref[...].astype(F32), (128, 128)).astype(BF)


def pack(flux, field, route_row):
    return pl.pallas_call(
        pack_kernel,
        grid=(1,),
        in_specs=[
            pl.BlockSpec((128, WAVES), lambda i: (0, 0)),
            pl.BlockSpec((None, 8, 8, 8, WAVES), lambda i: (2, 0, 0, 0, 0)),
            pl.BlockSpec((1, 128), lambda i: (0, 0)),
        ],
        out_specs=pl.BlockSpec((128, 2 * WAVES + 128), lambda i: (0, 0)),
        out_shape=jax.ShapeDtypeStruct((128, 2 * WAVES + 128), BF),
        scratch_shapes=[pltpu.VMEM((128, WAVES), F32)],
        compiler_params=pltpu.CompilerParams(vmem_limit_bytes=8 << 20),
        name="pack",
    )(in_hbm(flux), in_hbm(field), route_row)


def stencil_kernel(first, side_ref, mix_ref, *refs):
    if first:
        u_ref, sib, far, even, odd, st_ref, flux_ref, route_ref, out_ref, w_ref, wp_ref, f_sib, f_far, f_even, f_odd = refs
    else:
        u_ref, sib, far, even, odd, st_ref, out_ref = refs
    row_even = side_ref[0] == 0
    col_even = side_ref[1] == 0

    def low_x(c, y):
        return jnp.where(row_even, far[c, y], sib[c, y]).astype(F32)

    def high_x(c, y):
        return jnp.where(row_even, sib[c, y], far[c, y]).astype(F32)

    def low_y(c, x):
        return jnp.where(col_even, odd[c, x], even[c, x]).astype(F32)

    def high_y(c, x):
        return jnp.where(col_even, even[c, x], odd[c, x]).astype(F32)

    depth = lax.broadcasted_iota(jnp.int32, (8, LANES), 0)
    bottom = depth == 0
    top = depth == 7
    mix = [[mix_ref[i, j] for j in range(3)] for i in range(3)]

    def plane(x, below, above):
        for y in range(8):
            cell = [u_ref[c, x, y] for c in range(3)]
            stiff = jnp.broadcast_to(st_ref[x, y], (8, LANES))
            for c in range(3):
                u = cell[c]
                total = below(c, y) + above(c, y)
                total = total + (u_ref[c, x, y - 1] if y > 0 else low_y(c, x))
                total = total + (u_ref[c, x, y + 1] if y < 7 else high_y(c, x))
                total = total + jnp.where(bottom, 0.0, pltpu.roll(u, 1, 0))
                total = total + jnp.where(top, 0.0, pltpu.roll(u, 7, 0))
                mixed = mix[c][0] * cell[0] + mix[c][1] * cell[1] + mix[c][2] * cell[2]
                value = stiff * (u - total * (1.0 / 6.0)) + mixed
                if first and c == 2:
                    low = flux_ref[pl.ds(x * 8 + y, 1), :]
                    high = flux_ref[pl.ds(64 + x * 8 + y, 1), :]
                    value = value - jnp.where(bottom, low, jnp.where(top, high, 0.0))
                    w_ref[pl.ds(x * 8 + y, 1), :] = value[0:1]
                    w_ref[pl.ds(64 + x * 8 + y, 1), :] = value[7:8]
                out_ref[c, x, y] = value

    plane(0, low_x, lambda c, y: u_ref[c, 1, y])

    def step(x, carry):
        plane(x, lambda c, y: u_ref[c, x - 1, y], lambda c, y: u_ref[c, x + 1, y])
        return carry

    lax.fori_loop(1, 7, step, 0)
    plane(7, lambda c, y: u_ref[c, 6, y], high_x)
    if first:
        f_sib[...] = jnp.where(row_even, out_ref[:, 7], out_ref[:, 0]).astype(BF)
        f_far[...] = jnp.where(row_even, out_ref[:, 0], out_ref[:, 7]).astype(BF)
        f_even[...] = jnp.where(col_even, out_ref[:, :, 7], out_ref[:, :, 0]).astype(BF)
        f_odd[...] = jnp.where(col_even, out_ref[:, :, 0], out_ref[:, :, 7]).astype(BF)
        wp_ref[...] = jnp.dot(onehot(route_ref[...], 128), w_ref[...].astype(BF), preferred_element_type=F32).astype(BF)


def stencil(side, field, halos, stiffness, mixing, flux=None, route_row=None):
    first = flux is not None
    whole = pl.BlockSpec((3, 8, 8, 8, LANES), lambda i: (0, 0, 0, 0, i))
    face = pl.BlockSpec((3, 8, 8, LANES), lambda i: (0, 0, 0, i))
    panel = pl.BlockSpec((128, LANES), lambda i: (0, i))
    in_specs = [pl.BlockSpec(memory_space=pltpu.SMEM)] * 2 + [whole, face, face, face, face,
                pl.BlockSpec((8, 8, 8, 1), lambda i: (0, 0, 0, 0))]
    args = [side, mixing, in_hbm(field), *halos, stiffness]
    out_specs = [whole]
    out_shape = [pltpu.HBM(field.shape, F32)]
    if first:
        in_specs += [panel, pl.BlockSpec((1, 128), lambda i: (0, 0))]
        args += [flux, route_row]
        out_specs += [panel, panel, face, face, face, face]
        out_shape += [jax.ShapeDtypeStruct((128, WAVES), F32), jax.ShapeDtypeStruct((128, WAVES), BF)]
        out_shape += [jax.ShapeDtypeStruct((3, 8, 8, WAVES), BF)] * 4
    return pl.pallas_call(
        lambda *refs: stencil_kernel(first, *refs),
        grid=(WAVES // LANES,),
        in_specs=in_specs,
        out_specs=out_specs,
        out_shape=out_shape,
        compiler_params=pltpu.CompilerParams(vmem_limit_bytes=8 << 20),
        name="stencil_first" if first else "stencil_second",
    )(*args)


def boundary_kernel(first, order_ref, rows_ref, cols_ref, count_ref, *refs):
    chunks = refs[:8]
    single_ref, double_ref, near_ref = refs[8:11]
    extra_ref, *keys, out_ref, single_buf, double_buf, phi_ref, w_ref, acc_ref, sems = refs[11:]
    copies = []
    for i in range(2048 // ROWS):
        part = pl.ds(i * ROWS, ROWS)
        copies.append((
            pltpu.make_async_copy(single_ref.at[part], single_buf.at[part], sems.at[0, i]),
            pltpu.make_async_copy(double_ref.at[part], double_buf.at[part], sems.at[1, i]),
        ))
    for pair in copies:
        pair[0].start()
        pair[1].start()
    for k in range(8):
        at = pl.multiple_of(order_ref[k] * 128, 128)
        phi_ref[pl.ds(at, 128), :] = chunks[k][0]
        w_ref[pl.ds(at, 128), :] = chunks[k][1]
    m = lax.broadcasted_iota(jnp.int32, (256, 256), 0)
    place = (m // 16) * 8 + m % 8 + 128 * ((m // 8) % 2)

    for i in range(2048 // ROWS):
        part = pl.ds(i * ROWS, ROWS)
        copies[i][0].wait()
        far = jnp.dot(single_buf[part, :], phi_ref[...], preferred_element_type=F32)
        copies[i][1].wait()
        acc_ref[...] = far + jnp.dot(double_buf[part, :], w_ref[...], preferred_element_type=F32)

        def add_near(k, carry, i=i):
            @pl.when((k < count_ref[0]) & (rows_ref[k] // (ROWS // 128) == i))
            def _():
                row = pl.multiple_of((rows_ref[k] % (ROWS // 128)) * 128, 128)
                col = pl.multiple_of(cols_ref[k] * 128, 128)
                acc_ref[pl.ds(row, 128), :] += jnp.dot(
                    near_ref[k], phi_ref[pl.ds(col, 128), :], preferred_element_type=F32
                )

            return carry

        lax.fori_loop(0, 8, add_near, 0)
        total = acc_ref[...].astype(BF)
        if first:
            for p in range(ROWS // 256):
                pair = i * (ROWS // 256) + p
                select = (place == keys[0][pair]).astype(F32).astype(BF)
                packed = jnp.dot(select, total[p * 256 : p * 256 + 256], preferred_element_type=F32).astype(BF)
                out_ref[:, pair * 16 : pair * 16 + 16, :] = packed.reshape(16, 16, WAVES)
        else:
            owners = ROWS // 128
            out_ref[i * owners : (i + 1) * owners, 0:128, :] = total.reshape(owners, 128, WAVES)
    out_ref[:, 128:136, :] = extra_ref[...]


def boundary(order, near, chunks, single_layer, double_layer, extra, *keys):
    near_blocks, near_rows, near_cols, near_count = near
    first = len(keys) > 0
    vmem = pl.BlockSpec(memory_space=pltpu.VMEM)
    hbm = pl.BlockSpec(memory_space=pltpu.HBM)
    matrix = pltpu.VMEM((2048, 1024), BF)
    return pl.pallas_call(
        lambda *refs: boundary_kernel(first, *refs),
        in_specs=[pl.BlockSpec(memory_space=pltpu.SMEM)] * 4 + [vmem] * 8 + [hbm, hbm] + [vmem] * (2 + len(keys)),
        out_specs=vmem,
        out_shape=jax.ShapeDtypeStruct((16, 136, WAVES), BF),
        scratch_shapes=[
            matrix,
            matrix,
            pltpu.VMEM((1024, WAVES), BF),
            pltpu.VMEM((1024, WAVES), BF),
            pltpu.VMEM((ROWS, WAVES), F32),
            pltpu.SemaphoreType.DMA((2, 2048 // ROWS)),
        ],
        compiler_params=pltpu.CompilerParams(vmem_limit_bytes=LIMIT << 20),
        name="boundary_first" if first else "boundary_second",
    )(order, near_rows, near_cols, near_count, *chunks, in_hbm(single_layer), in_hbm(double_layer), near_blocks, extra, *keys)


def faces_kernel(side_ref, low_x, high_x, low_y, high_y, sib, far, even, odd):
    row_even = side_ref[0] == 0
    col_even = side_ref[1] == 0
    sib[...] = jnp.where(row_even, high_x[...], low_x[...]).astype(BF)
    far[...] = jnp.where(row_even, low_x[...], high_x[...]).astype(BF)
    even[...] = jnp.where(col_even, high_y[...], low_y[...]).astype(BF)
    odd[...] = jnp.where(col_even, low_y[...], high_y[...]).astype(BF)


def faces_of(side, field):
    across = lambda at: pl.BlockSpec((3, None, 8, 8, WAVES), lambda i: (0, at, 0, 0, 0))
    along = lambda at: pl.BlockSpec((3, 8, None, 8, WAVES), lambda i: (0, 0, at, 0, 0))
    out = pl.BlockSpec((3, 8, 8, WAVES), lambda i: (0, 0, 0, 0))
    return pl.pallas_call(
        faces_kernel,
        grid=(1,),
        in_specs=[pl.BlockSpec(memory_space=pltpu.SMEM), across(0), across(7), along(0), along(7)],
        out_specs=[out] * 4,
        out_shape=[jax.ShapeDtypeStruct((3, 8, 8, WAVES), BF)] * 4,
        compiler_params=pltpu.CompilerParams(vmem_limit_bytes=8 << 20),
        name="faces",
    )(side, *[in_hbm(field)] * 4)


def middle_kernel(got_ref, chunk_ref, out_ref):
    total = got_ref[0, 0:128].astype(F32)
    for k in range(1, 16):
        total = total + got_ref[k, 0:128].astype(F32)
    out_ref[0] = (total - 0.5 * chunk_ref[...].astype(F32)).astype(BF)
    out_ref[1] = got_ref[:, 128:136, :].reshape(128, LANES)


def middle(got, chunk):
    return pl.pallas_call(
        middle_kernel,
        grid=(WAVES // LANES,),
        in_specs=[
            pl.BlockSpec((16, 136, LANES), lambda i: (0, 0, i)),
            pl.BlockSpec((None, 128, LANES), lambda i: (1, 0, i)),
        ],
        out_specs=pl.BlockSpec((2, 128, LANES), lambda i: (0, 0, i)),
        out_shape=jax.ShapeDtypeStruct((2, 128, WAVES), BF),
        compiler_params=pltpu.CompilerParams(vmem_limit_bytes=8 << 20),
        name="middle",
    )(got, chunk)


def last_kernel(got_ref, w_ref, route_ref, comp_ref, flux_ref, out_ref, mid_ref):
    total = got_ref[0, 0:128].astype(F32)
    for k in range(1, 16):
        total = total + got_ref[k, 0:128].astype(F32)
    flux_ref[...] = total - 0.5 * w_ref[...]
    picker = (lax.broadcasted_iota(jnp.int32, (128, 128), 1) == route_ref[...]).astype(F32).astype(BF)
    mid_ref[...] = jnp.dot(picker, got_ref[:, 128:136, :].reshape(128, LANES), preferred_element_type=F32)
    depth = lax.broadcasted_iota(jnp.int32, (8, LANES), 0)

    def step(x, carry):
        for y in range(8):
            low = mid_ref[pl.ds(x * 8 + y, 1), :]
            high = mid_ref[pl.ds(64 + x * 8 + y, 1), :]
            out_ref[x, y] = comp_ref[x, y] - jnp.where(depth == 0, low, jnp.where(depth == 7, high, 0.0))
        return carry

    lax.fori_loop(0, 8, step, 0)


def last(got, trace, route_column, field):
    comp = pl.BlockSpec((None, 8, 8, 8, LANES), lambda i: (2, 0, 0, 0, i))
    panel = pl.BlockSpec((128, LANES), lambda i: (0, i))
    return pl.pallas_call(
        last_kernel,
        grid=(WAVES // LANES,),
        in_specs=[
            pl.BlockSpec((16, 136, LANES), lambda i: (0, 0, i)),
            panel,
            pl.BlockSpec((128, 1), lambda i: (0, 0)),
            comp,
        ],
        out_specs=[panel, comp],
        out_shape=[jax.ShapeDtypeStruct((128, WAVES), F32), jax.ShapeDtypeStruct(field.shape, F32)],
        scratch_shapes=[pltpu.VMEM((128, LANES), F32)],
        input_output_aliases={3: 1},
        compiler_params=pltpu.CompilerParams(vmem_limit_bytes=8 << 20),
        name="last",
    )(got, trace, route_column, in_hbm(field))


def shifted(count, by):
    return [(i, (i + by) % count) for i in range(count)]


def in_hbm(array):
    return pltpu.with_memory_space_constraint(array, pltpu.HBM)


def swapped(count, bits):
    return [(i, i ^ bits) for i in range(count)]


def across_rows(chunk):
    mine = [chunk] + [lax.ppermute(chunk, "row", swapped(8, k)) for k in (4, 2, 6)]
    beside = [lax.ppermute(one, "row", swapped(8, 1)) for one in mine]
    order = lax.axis_index("row") ^ jnp.array([0, 4, 2, 6, 1, 5, 3, 7], jnp.int32)
    return mine + beside, order


def swap_faces(sib, far, even, odd):
    across = lambda count: [pair for i in range(1, count - 1, 2) for pair in ((i, i + 1), (i + 1, i))]
    return (
        lax.ppermute(sib, "row", swapped(8, 1)),
        lax.ppermute(far, "row", across(8)),
        lax.ppermute(even, "col", swapped(16, 1)),
        lax.ppermute(odd, "col", across(16)),
    )


def after(value, *others):
    return lax.optimization_barrier((value, *others))[0]


def local(
    displacement,
    flux,
    stiffness,
    mixing,
    single_layer,
    double_layer,
    near_blocks,
    near_rows,
    near_cols,
    near_counts,
    routes,
):
    near = (near_blocks.reshape(8, 128, 128), near_rows.reshape(8), near_cols.reshape(8), near_counts.reshape(1))
    route_row = routes.reshape(1, 128)
    side = jnp.stack([lax.axis_index("row") % 2, lax.axis_index("col") % 2]).astype(jnp.int32)
    stiff = stiffness[..., None]

    packed = pack(flux, displacement, route_row)
    got = lax.all_to_all(packed.reshape(16, 8, 2 * WAVES + 128), "col", 0, 0, tiled=True)
    halos = swap_faces(*faces_of(side, displacement))
    chunk = jnp.stack(
        [got[:, :, :WAVES].reshape(128, WAVES), got[:, :, WAVES : 2 * WAVES].reshape(128, WAVES)], 0
    )
    keys = got[:, 0, 2 * WAVES :].astype(jnp.int32).reshape(8, 2, 128)
    keys = (keys + jnp.array([0, 128], jnp.int32)[None, :, None]).reshape(8, 1, 256)

    field, trace, outgoing, *faces = stencil(side, displacement, halos, stiff, mixing, flux, route_row)
    chunks, order = across_rows(chunk)
    sums = boundary(order, near, chunks, single_layer, double_layer, outgoing.reshape(16, 8, WAVES), keys)
    got = lax.all_to_all(sums, "col", 0, 0, tiled=True)
    halos = swap_faces(*after(faces, sums))
    chunk = middle(after(got, halos), chunk)

    chunks, order = across_rows(chunk)
    sums = boundary(order, near, chunks, single_layer, double_layer, chunk[0].reshape(16, 8, WAVES))
    got = lax.all_to_all(sums, "col", 0, 0, tiled=True)
    (field,) = stencil(side, field, after(halos, sums), stiff, mixing)
    new_flux, field = last(after(got, field), trace, routes.reshape(128, 1), field)
    return (field, new_flux)


def solution(mesh):
    return jax.shard_map(
        local,
        mesh=mesh,
        in_specs=(
            P(None, "row", "col", None, None),
            P(("row", "col"), None),
            P("row", "col", None),
            P(),
            P("row", "col"),
            P("row", "col"),
            P("row", "col", None, None),
            P("row", "col"),
            P("row", "col"),
            P("row", "col"),
            P(("row", "col")),
        ),
        out_specs=(P(None, "row", "col", None, None), P(("row", "col"), None)),
        check_vma=False,
    )
```

```python
import jax
import jax.numpy as jnp
from jax import lax
from jax.experimental import pallas as pl
from jax.experimental.pallas import tpu as pltpu
from jax.sharding import PartitionSpec as P

BF = jnp.bfloat16
F32 = jnp.float32
WAVES = 384
LANES = 128
ROWS = 512
LIMIT = 12


def onehot(keys, count):
    rows = lax.broadcasted_iota(jnp.int32, (count, keys.shape[1]), 0)
    return (rows == keys).astype(F32).astype(BF)


def pack_kernel(flux_ref, comp_ref, route_ref, out_ref, trace_ref):
    by_panel = onehot(route_ref[...], 128)
    out_ref[:, 0:WAVES] = jnp.dot(by_panel, flux_ref[...].astype(BF), preferred_element_type=F32).astype(BF)

    def step(x, carry):
        for y in range(8):
            trace_ref[pl.ds(x * 8 + y, 1), :] = comp_ref[x, y, 0:1]
            trace_ref[pl.ds(64 + x * 8 + y, 1), :] = comp_ref[x, y, 7:8]
        return carry

    lax.fori_loop(0, 8, step, 0)
    out_ref[:, WAVES : 2 * WAVES] = jnp.dot(
        by_panel, trace_ref[...].astype(BF), preferred_element_type=F32
    ).astype(BF)
    out_ref[:, 2 * WAVES :] = jnp.broadcast_to(route_ref[...].astype(F32), (128, 128)).astype(BF)


def pack(flux, field, route_row):
    return pl.pallas_call(
        pack_kernel,
        grid=(1,),
        in_specs=[
            pl.BlockSpec((128, WAVES), lambda i: (0, 0)),
            pl.BlockSpec((None, 8, 8, 8, WAVES), lambda i: (2, 0, 0, 0, 0)),
            pl.BlockSpec((1, 128), lambda i: (0, 0)),
        ],
        out_specs=pl.BlockSpec((128, 2 * WAVES + 128), lambda i: (0, 0)),
        out_shape=jax.ShapeDtypeStruct((128, 2 * WAVES + 128), BF),
        scratch_shapes=[pltpu.VMEM((128, WAVES), F32)],
        compiler_params=pltpu.CompilerParams(vmem_limit_bytes=8 << 20),
        name="pack",
    )(in_hbm(flux), in_hbm(field), route_row)


def stencil_kernel(first, side_ref, mix_ref, *refs):
    if first:
        u_ref, sib, far, even, odd, st_ref, flux_ref, route_ref, out_ref, w_ref, wp_ref, f_sib, f_far, f_even, f_odd = refs
    else:
        u_ref, sib, far, even, odd, st_ref, out_ref = refs
    row_even = side_ref[0] == 0
    col_even = side_ref[1] == 0

    def low_x(c, y):
        return jnp.where(row_even, far[c, y], sib[c, y]).astype(F32)

    def high_x(c, y):
        return jnp.where(row_even, sib[c, y], far[c, y]).astype(F32)

    def low_y(c, x):
        return jnp.where(col_even, odd[c, x], even[c, x]).astype(F32)

    def high_y(c, x):
        return jnp.where(col_even, even[c, x], odd[c, x]).astype(F32)

    depth = lax.broadcasted_iota(jnp.int32, (8, LANES), 0)
    bottom = depth == 0
    top = depth == 7
    mix = [[mix_ref[i, j] for j in range(3)] for i in range(3)]

    def plane(x, below, above):
        for y in range(8):
            cell = [u_ref[c, x, y] for c in range(3)]
            stiff = jnp.broadcast_to(st_ref[x, y], (8, LANES))
            for c in range(3):
                u = cell[c]
                total = below(c, y) + above(c, y)
                total = total + (u_ref[c, x, y - 1] if y > 0 else low_y(c, x))
                total = total + (u_ref[c, x, y + 1] if y < 7 else high_y(c, x))
                total = total + jnp.where(bottom, 0.0, pltpu.roll(u, 1, 0))
                total = total + jnp.where(top, 0.0, pltpu.roll(u, 7, 0))
                mixed = mix[c][0] * cell[0] + mix[c][1] * cell[1] + mix[c][2] * cell[2]
                value = stiff * (u - total * (1.0 / 6.0)) + mixed
                if first and c == 2:
                    low = flux_ref[pl.ds(x * 8 + y, 1), :]
                    high = flux_ref[pl.ds(64 + x * 8 + y, 1), :]
                    value = value - jnp.where(bottom, low, jnp.where(top, high, 0.0))
                    w_ref[pl.ds(x * 8 + y, 1), :] = value[0:1]
                    w_ref[pl.ds(64 + x * 8 + y, 1), :] = value[7:8]
                out_ref[c, x, y] = value

    plane(0, low_x, lambda c, y: u_ref[c, 1, y])

    def step(x, carry):
        plane(x, lambda c, y: u_ref[c, x - 1, y], lambda c, y: u_ref[c, x + 1, y])
        return carry

    lax.fori_loop(1, 7, step, 0)
    plane(7, lambda c, y: u_ref[c, 6, y], high_x)
    if first:
        f_sib[...] = jnp.where(row_even, out_ref[:, 7], out_ref[:, 0]).astype(BF)
        f_far[...] = jnp.where(row_even, out_ref[:, 0], out_ref[:, 7]).astype(BF)
        f_even[...] = jnp.where(col_even, out_ref[:, :, 7], out_ref[:, :, 0]).astype(BF)
        f_odd[...] = jnp.where(col_even, out_ref[:, :, 0], out_ref[:, :, 7]).astype(BF)
        wp_ref[...] = jnp.dot(onehot(route_ref[...], 128), w_ref[...].astype(BF), preferred_element_type=F32).astype(BF)


def stencil(side, field, halos, stiffness, mixing, flux=None, route_row=None):
    first = flux is not None
    whole = pl.BlockSpec((3, 8, 8, 8, LANES), lambda i: (0, 0, 0, 0, i))
    face = pl.BlockSpec((3, 8, 8, LANES), lambda i: (0, 0, 0, i))
    panel = pl.BlockSpec((128, LANES), lambda i: (0, i))
    in_specs = [pl.BlockSpec(memory_space=pltpu.SMEM)] * 2 + [whole, face, face, face, face,
                pl.BlockSpec((8, 8, 8, 1), lambda i: (0, 0, 0, 0))]
    args = [side, mixing, in_hbm(field), *halos, stiffness]
    out_specs = [whole]
    out_shape = [pltpu.HBM(field.shape, F32)]
    if first:
        in_specs += [panel, pl.BlockSpec((1, 128), lambda i: (0, 0))]
        args += [flux, route_row]
        out_specs += [panel, panel, face, face, face, face]
        out_shape += [jax.ShapeDtypeStruct((128, WAVES), F32), jax.ShapeDtypeStruct((128, WAVES), BF)]
        out_shape += [jax.ShapeDtypeStruct((3, 8, 8, WAVES), BF)] * 4
    return pl.pallas_call(
        lambda *refs: stencil_kernel(first, *refs),
        grid=(WAVES // LANES,),
        in_specs=in_specs,
        out_specs=out_specs,
        out_shape=out_shape,
        compiler_params=pltpu.CompilerParams(vmem_limit_bytes=8 << 20),
        name="stencil_first" if first else "stencil_second",
    )(*args)


def stage_kernel(side_ref, single_hbm, double_hbm, single_ref, double_ref, sems):
    copies = [
        pltpu.make_async_copy(single_hbm, single_ref, sems.at[0]),
        pltpu.make_async_copy(double_hbm, double_ref, sems.at[1]),
    ]
    for copy in copies:
        copy.start()
    for copy in copies:
        copy.wait()


def stage(side, single_layer, double_layer):
    hbm = pl.BlockSpec(memory_space=pltpu.HBM)
    return pl.pallas_call(
        stage_kernel,
        in_specs=[pl.BlockSpec(memory_space=pltpu.SMEM), hbm, hbm],
        out_specs=[pl.BlockSpec(memory_space=pltpu.VMEM)] * 2,
        out_shape=[pltpu.VMEM((2048, 1024), BF)] * 2,
        scratch_shapes=[pltpu.SemaphoreType.DMA((2,))],
        compiler_params=pltpu.CompilerParams(vmem_limit_bytes=10 << 20),
        name="stage",
    )(side, in_hbm(single_layer), in_hbm(double_layer))


def boundary_kernel(first, order_ref, rows_ref, cols_ref, count_ref, *refs):
    chunks = refs[:8]
    single_ref, double_ref, near_ref = refs[8:11]
    extra_ref, *keys, out_ref, phi_ref, w_ref, acc_ref = refs[11:]
    for k in range(8):
        at = pl.multiple_of(order_ref[k] * 128, 128)
        phi_ref[pl.ds(at, 128), :] = chunks[k][0]
        w_ref[pl.ds(at, 128), :] = chunks[k][1]
    m = lax.broadcasted_iota(jnp.int32, (256, 256), 0)
    place = (m // 16) * 8 + m % 8 + 128 * ((m // 8) % 2)

    for i in range(2048 // ROWS):
        part = pl.ds(i * ROWS, ROWS)
        acc_ref[...] = jnp.dot(single_ref[part, :], phi_ref[...], preferred_element_type=F32) + jnp.dot(
            double_ref[part, :], w_ref[...], preferred_element_type=F32
        )

        def add_near(k, carry, i=i):
            @pl.when((k < count_ref[0]) & (rows_ref[k] // (ROWS // 128) == i))
            def _():
                row = pl.multiple_of((rows_ref[k] % (ROWS // 128)) * 128, 128)
                col = pl.multiple_of(cols_ref[k] * 128, 128)
                acc_ref[pl.ds(row, 128), :] += jnp.dot(
                    near_ref[k], phi_ref[pl.ds(col, 128), :], preferred_element_type=F32
                )

            return carry

        lax.fori_loop(0, 8, add_near, 0)
        total = acc_ref[...].astype(BF)
        if first:
            for p in range(ROWS // 256):
                pair = i * (ROWS // 256) + p
                select = (place == keys[0][pair]).astype(F32).astype(BF)
                packed = jnp.dot(select, total[p * 256 : p * 256 + 256], preferred_element_type=F32).astype(BF)
                out_ref[:, pair * 16 : pair * 16 + 16, :] = packed.reshape(16, 16, WAVES)
        else:
            owners = ROWS // 128
            out_ref[i * owners : (i + 1) * owners, 0:128, :] = total.reshape(owners, 128, WAVES)
    out_ref[:, 128:136, :] = extra_ref[...]


def boundary(order, near, chunks, matrices, extra, *keys):
    near_blocks, near_rows, near_cols, near_count = near
    first = len(keys) > 0
    vmem = pl.BlockSpec(memory_space=pltpu.VMEM)
    return pl.pallas_call(
        lambda *refs: boundary_kernel(first, *refs),
        in_specs=[pl.BlockSpec(memory_space=pltpu.SMEM)] * 4 + [vmem] * (12 + len(keys)),
        out_specs=vmem,
        out_shape=jax.ShapeDtypeStruct((16, 136, WAVES), BF),
        scratch_shapes=[
            pltpu.VMEM((1024, WAVES), BF),
            pltpu.VMEM((1024, WAVES), BF),
            pltpu.VMEM((ROWS, WAVES), F32),
        ],
        compiler_params=pltpu.CompilerParams(vmem_limit_bytes=LIMIT << 20),
        name="boundary_first" if first else "boundary_second",
    )(order, near_rows, near_cols, near_count, *chunks, *matrices, near_blocks, extra, *keys)


def faces_kernel(side_ref, low_x, high_x, low_y, high_y, sib, far, even, odd):
    row_even = side_ref[0] == 0
    col_even = side_ref[1] == 0
    sib[...] = jnp.where(row_even, high_x[...], low_x[...]).astype(BF)
    far[...] = jnp.where(row_even, low_x[...], high_x[...]).astype(BF)
    even[...] = jnp.where(col_even, high_y[...], low_y[...]).astype(BF)
    odd[...] = jnp.where(col_even, low_y[...], high_y[...]).astype(BF)


def faces_of(side, field):
    across = lambda at: pl.BlockSpec((3, None, 8, 8, WAVES), lambda i: (0, at, 0, 0, 0))
    along = lambda at: pl.BlockSpec((3, 8, None, 8, WAVES), lambda i: (0, 0, at, 0, 0))
    out = pl.BlockSpec((3, 8, 8, WAVES), lambda i: (0, 0, 0, 0))
    return pl.pallas_call(
        faces_kernel,
        grid=(1,),
        in_specs=[pl.BlockSpec(memory_space=pltpu.SMEM), across(0), across(7), along(0), along(7)],
        out_specs=[out] * 4,
        out_shape=[jax.ShapeDtypeStruct((3, 8, 8, WAVES), BF)] * 4,
        compiler_params=pltpu.CompilerParams(vmem_limit_bytes=8 << 20),
        name="faces",
    )(side, *[in_hbm(field)] * 4)


def middle_kernel(got_ref, chunk_ref, out_ref):
    total = got_ref[0, 0:128].astype(F32)
    for k in range(1, 16):
        total = total + got_ref[k, 0:128].astype(F32)
    out_ref[0] = (total - 0.5 * chunk_ref[...].astype(F32)).astype(BF)
    out_ref[1] = got_ref[:, 128:136, :].reshape(128, LANES)


def middle(got, chunk):
    return pl.pallas_call(
        middle_kernel,
        grid=(WAVES // LANES,),
        in_specs=[
            pl.BlockSpec((16, 136, LANES), lambda i: (0, 0, i)),
            pl.BlockSpec((None, 128, LANES), lambda i: (1, 0, i)),
        ],
        out_specs=pl.BlockSpec((2, 128, LANES), lambda i: (0, 0, i)),
        out_shape=jax.ShapeDtypeStruct((2, 128, WAVES), BF),
        compiler_params=pltpu.CompilerParams(vmem_limit_bytes=8 << 20),
        name="middle",
    )(got, chunk)


def last_kernel(got_ref, w_ref, route_ref, comp_ref, flux_ref, out_ref, mid_ref):
    total = got_ref[0, 0:128].astype(F32)
    for k in range(1, 16):
        total = total + got_ref[k, 0:128].astype(F32)
    flux_ref[...] = total - 0.5 * w_ref[...]
    picker = (lax.broadcasted_iota(jnp.int32, (128, 128), 1) == route_ref[...]).astype(F32).astype(BF)
    mid_ref[...] = jnp.dot(picker, got_ref[:, 128:136, :].reshape(128, LANES), preferred_element_type=F32)
    depth = lax.broadcasted_iota(jnp.int32, (8, LANES), 0)

    def step(x, carry):
        for y in range(8):
            low = mid_ref[pl.ds(x * 8 + y, 1), :]
            high = mid_ref[pl.ds(64 + x * 8 + y, 1), :]
            out_ref[x, y] = comp_ref[x, y] - jnp.where(depth == 0, low, jnp.where(depth == 7, high, 0.0))
        return carry

    lax.fori_loop(0, 8, step, 0)


def last(got, trace, route_column, field):
    comp = pl.BlockSpec((None, 8, 8, 8, LANES), lambda i: (2, 0, 0, 0, i))
    panel = pl.BlockSpec((128, LANES), lambda i: (0, i))
    return pl.pallas_call(
        last_kernel,
        grid=(WAVES // LANES,),
        in_specs=[
            pl.BlockSpec((16, 136, LANES), lambda i: (0, 0, i)),
            panel,
            pl.BlockSpec((128, 1), lambda i: (0, 0)),
            comp,
        ],
        out_specs=[panel, comp],
        out_shape=[jax.ShapeDtypeStruct((128, WAVES), F32), jax.ShapeDtypeStruct(field.shape, F32)],
        scratch_shapes=[pltpu.VMEM((128, LANES), F32)],
        input_output_aliases={3: 1},
        compiler_params=pltpu.CompilerParams(vmem_limit_bytes=8 << 20),
        name="last",
    )(got, trace, route_column, in_hbm(field))


def shifted(count, by):
    return [(i, (i + by) % count) for i in range(count)]


def in_hbm(array):
    return pltpu.with_memory_space_constraint(array, pltpu.HBM)


def swapped(count, bits):
    return [(i, i ^ bits) for i in range(count)]


def across_rows(chunk):
    mine = [chunk] + [lax.ppermute(chunk, "row", swapped(8, k)) for k in (4, 2, 6)]
    beside = [lax.ppermute(one, "row", swapped(8, 1)) for one in mine]
    order = lax.axis_index("row") ^ jnp.array([0, 4, 2, 6, 1, 5, 3, 7], jnp.int32)
    return mine + beside, order


def swap_faces(sib, far, even, odd):
    across = lambda count: [pair for i in range(1, count - 1, 2) for pair in ((i, i + 1), (i + 1, i))]
    return (
        lax.ppermute(sib, "row", swapped(8, 1)),
        lax.ppermute(far, "row", across(8)),
        lax.ppermute(even, "col", swapped(16, 1)),
        lax.ppermute(odd, "col", across(16)),
    )


def after(value, *others):
    return lax.optimization_barrier((value, *others))[0]


def local(
    displacement,
    flux,
    stiffness,
    mixing,
    single_layer,
    double_layer,
    near_blocks,
    near_rows,
    near_cols,
    near_counts,
    routes,
):
    near = (near_blocks.reshape(8, 128, 128), near_rows.reshape(8), near_cols.reshape(8), near_counts.reshape(1))
    route_row = routes.reshape(1, 128)
    side = jnp.stack([lax.axis_index("row") % 2, lax.axis_index("col") % 2]).astype(jnp.int32)
    stiff = stiffness[..., None]

    packed = pack(flux, displacement, route_row)
    got = lax.all_to_all(packed.reshape(16, 8, 2 * WAVES + 128), "col", 0, 0, tiled=True)
    halos = swap_faces(*faces_of(side, displacement))
    field, trace, outgoing, *faces = stencil(side, displacement, halos, stiff, mixing, flux, route_row)
    got = after(got, outgoing)
    chunk = jnp.stack(
        [got[:, :, :WAVES].reshape(128, WAVES), got[:, :, WAVES : 2 * WAVES].reshape(128, WAVES)], 0
    )
    keys = got[:, 0, 2 * WAVES :].astype(jnp.int32).reshape(8, 2, 128)
    keys = (keys + jnp.array([0, 128], jnp.int32)[None, :, None]).reshape(8, 1, 256)

    matrices = stage(after(side, chunk), single_layer, double_layer)
    chunks, order = across_rows(chunk)
    sums = boundary(order, near, chunks, matrices, outgoing.reshape(16, 8, WAVES), keys)
    got = lax.all_to_all(sums, "col", 0, 0, tiled=True)
    halos = swap_faces(*after(faces, sums))
    chunk = middle(after(got, halos), chunk)
    matrices = stage(after(side, chunk), single_layer, double_layer)

    chunks, order = across_rows(chunk)
    sums = boundary(order, near, chunks, matrices, chunk[0].reshape(16, 8, WAVES))
    got = lax.all_to_all(sums, "col", 0, 0, tiled=True)
    (field,) = stencil(side, field, after(halos, sums), stiff, mixing)
    new_flux, field = last(after(got, field), trace, routes.reshape(128, 1), field)
    return (field, new_flux)


def solution(mesh):
    return jax.shard_map(
        local,
        mesh=mesh,
        in_specs=(
            P(None, "row", "col", None, None),
            P(("row", "col"), None),
            P("row", "col", None),
            P(),
            P("row", "col"),
            P("row", "col"),
            P("row", "col", None, None),
            P("row", "col"),
            P("row", "col"),
            P("row", "col"),
            P(("row", "col")),
        ),
        out_specs=(P(None, "row", "col", None, None), P(("row", "col"), None)),
        check_vma=False,
    )
```

```python
import jax
import jax.numpy as jnp
from jax import lax
from jax.experimental import pallas as pl
from jax.experimental.pallas import tpu as pltpu
from jax.sharding import PartitionSpec as P

BF = jnp.bfloat16
F32 = jnp.float32
WAVES = 384
LANES = 128
ROWS = 512
LIMIT = 12


def onehot(keys, count):
    rows = lax.broadcasted_iota(jnp.int32, (count, keys.shape[1]), 0)
    return (rows == keys).astype(F32).astype(BF)


def pack_kernel(flux_ref, comp_ref, route_ref, out_ref, trace_ref):
    by_panel = onehot(route_ref[...], 128)
    out_ref[:, 0:WAVES] = jnp.dot(by_panel, flux_ref[...].astype(BF), preferred_element_type=F32).astype(BF)

    def step(x, carry):
        for y in range(8):
            trace_ref[pl.ds(x * 8 + y, 1), :] = comp_ref[x, y, 0:1]
            trace_ref[pl.ds(64 + x * 8 + y, 1), :] = comp_ref[x, y, 7:8]
        return carry

    lax.fori_loop(0, 8, step, 0)
    out_ref[:, WAVES : 2 * WAVES] = jnp.dot(
        by_panel, trace_ref[...].astype(BF), preferred_element_type=F32
    ).astype(BF)
    out_ref[:, 2 * WAVES :] = jnp.broadcast_to(route_ref[...].astype(F32), (128, 128)).astype(BF)


def pack(flux, field, route_row):
    return pl.pallas_call(
        pack_kernel,
        grid=(1,),
        in_specs=[
            pl.BlockSpec((128, WAVES), lambda i: (0, 0)),
            pl.BlockSpec((None, 8, 8, 8, WAVES), lambda i: (2, 0, 0, 0, 0)),
            pl.BlockSpec((1, 128), lambda i: (0, 0)),
        ],
        out_specs=pl.BlockSpec((128, 2 * WAVES + 128), lambda i: (0, 0)),
        out_shape=jax.ShapeDtypeStruct((128, 2 * WAVES + 128), BF),
        scratch_shapes=[pltpu.VMEM((128, WAVES), F32)],
        compiler_params=pltpu.CompilerParams(vmem_limit_bytes=8 << 20),
        name="pack",
    )(in_hbm(flux), in_hbm(field), route_row)


def stencil_kernel(first, side_ref, mix_ref, *refs):
    if first:
        u_ref, sib, far, even, odd, st_ref, flux_ref, route_ref, out_ref, w_ref, wp_ref, f_sib, f_far, f_even, f_odd = refs
    else:
        u_ref, sib, far, even, odd, st_ref, out_ref, comp_ref = refs
    row_even = side_ref[0] == 0
    col_even = side_ref[1] == 0

    def low_x(c, y):
        return jnp.where(row_even, far[c, y], sib[c, y]).astype(F32)

    def high_x(c, y):
        return jnp.where(row_even, sib[c, y], far[c, y]).astype(F32)

    def low_y(c, x):
        return jnp.where(col_even, odd[c, x], even[c, x]).astype(F32)

    def high_y(c, x):
        return jnp.where(col_even, even[c, x], odd[c, x]).astype(F32)

    depth = lax.broadcasted_iota(jnp.int32, (8, LANES), 0)
    bottom = depth == 0
    top = depth == 7
    mix = [[mix_ref[i, j] for j in range(3)] for i in range(3)]

    def plane(x, below, above):
        for y in range(8):
            cell = [u_ref[c, x, y] for c in range(3)]
            stiff = jnp.broadcast_to(st_ref[x, y], (8, LANES))
            for c in range(3):
                u = cell[c]
                total = below(c, y) + above(c, y)
                total = total + (u_ref[c, x, y - 1] if y > 0 else low_y(c, x))
                total = total + (u_ref[c, x, y + 1] if y < 7 else high_y(c, x))
                total = total + jnp.where(bottom, 0.0, pltpu.roll(u, 1, 0))
                total = total + jnp.where(top, 0.0, pltpu.roll(u, 7, 0))
                mixed = mix[c][0] * cell[0] + mix[c][1] * cell[1] + mix[c][2] * cell[2]
                value = stiff * (u - total * (1.0 / 6.0)) + mixed
                if first and c == 2:
                    low = flux_ref[pl.ds(x * 8 + y, 1), :]
                    high = flux_ref[pl.ds(64 + x * 8 + y, 1), :]
                    value = value - jnp.where(bottom, low, jnp.where(top, high, 0.0))
                    w_ref[pl.ds(x * 8 + y, 1), :] = value[0:1]
                    w_ref[pl.ds(64 + x * 8 + y, 1), :] = value[7:8]
                if first or c < 2:
                    out_ref[c, x, y] = value
                else:
                    comp_ref[x, y] = value

    plane(0, low_x, lambda c, y: u_ref[c, 1, y])

    def step(x, carry):
        plane(x, lambda c, y: u_ref[c, x - 1, y], lambda c, y: u_ref[c, x + 1, y])
        return carry

    lax.fori_loop(1, 7, step, 0)
    plane(7, lambda c, y: u_ref[c, 6, y], high_x)
    if first:
        f_sib[...] = jnp.where(row_even, out_ref[:, 7], out_ref[:, 0]).astype(BF)
        f_far[...] = jnp.where(row_even, out_ref[:, 0], out_ref[:, 7]).astype(BF)
        f_even[...] = jnp.where(col_even, out_ref[:, :, 7], out_ref[:, :, 0]).astype(BF)
        f_odd[...] = jnp.where(col_even, out_ref[:, :, 0], out_ref[:, :, 7]).astype(BF)
        wp_ref[...] = jnp.dot(onehot(route_ref[...], 128), w_ref[...].astype(BF), preferred_element_type=F32).astype(BF)


def stencil(side, field, halos, stiffness, mixing, flux=None, route_row=None):
    first = flux is not None
    whole = pl.BlockSpec((3, 8, 8, 8, LANES), lambda i: (0, 0, 0, 0, i))
    face = pl.BlockSpec((3, 8, 8, LANES), lambda i: (0, 0, 0, i))
    panel = pl.BlockSpec((128, LANES), lambda i: (0, i))
    in_specs = [pl.BlockSpec(memory_space=pltpu.SMEM)] * 2 + [whole, face, face, face, face,
                pl.BlockSpec((8, 8, 8, 1), lambda i: (0, 0, 0, 0))]
    args = [side, mixing, in_hbm(field), *halos, stiffness]
    out_specs = [whole if first else pl.BlockSpec((2, 8, 8, 8, LANES), lambda i: (0, 0, 0, 0, i))]
    out_shape = [pltpu.HBM(field.shape, F32)]
    if not first:
        out_specs += [pl.BlockSpec((8, 8, 8, LANES), lambda i: (0, 0, 0, i))]
        out_shape += [jax.ShapeDtypeStruct(field.shape[1:], F32)]
    if first:
        in_specs += [panel, pl.BlockSpec((1, 128), lambda i: (0, 0))]
        args += [flux, route_row]
        out_specs += [panel, panel, face, face, face, face]
        out_shape += [jax.ShapeDtypeStruct((128, WAVES), F32), jax.ShapeDtypeStruct((128, WAVES), BF)]
        out_shape += [jax.ShapeDtypeStruct((3, 8, 8, WAVES), BF)] * 4
    return pl.pallas_call(
        lambda *refs: stencil_kernel(first, *refs),
        grid=(WAVES // LANES,),
        in_specs=in_specs,
        out_specs=out_specs,
        out_shape=out_shape,
        compiler_params=pltpu.CompilerParams(vmem_limit_bytes=8 << 20),
        name="stencil_first" if first else "stencil_second",
    )(*args)


def stage_kernel(side_ref, single_hbm, double_hbm, single_ref, double_ref, sems):
    copies = [
        pltpu.make_async_copy(single_hbm, single_ref, sems.at[0]),
        pltpu.make_async_copy(double_hbm, double_ref, sems.at[1]),
    ]
    for copy in copies:
        copy.start()
    for copy in copies:
        copy.wait()


def stage(side, single_layer, double_layer):
    hbm = pl.BlockSpec(memory_space=pltpu.HBM)
    return pl.pallas_call(
        stage_kernel,
        in_specs=[pl.BlockSpec(memory_space=pltpu.SMEM), hbm, hbm],
        out_specs=[pl.BlockSpec(memory_space=pltpu.VMEM)] * 2,
        out_shape=[pltpu.VMEM((2048, 1024), BF)] * 2,
        scratch_shapes=[pltpu.SemaphoreType.DMA((2,))],
        compiler_params=pltpu.CompilerParams(vmem_limit_bytes=10 << 20),
        name="stage",
    )(side, in_hbm(single_layer), in_hbm(double_layer))


def boundary_kernel(first, order_ref, rows_ref, cols_ref, count_ref, *refs):
    chunks = refs[:8]
    single_ref, double_ref, near_ref = refs[8:11]
    extra_ref, *keys, out_ref, phi_ref, w_ref, acc_ref = refs[11:]
    for k in range(8):
        at = pl.multiple_of(order_ref[k] * 128, 128)
        phi_ref[pl.ds(at, 128), :] = chunks[k][0]
        w_ref[pl.ds(at, 128), :] = chunks[k][1]
    m = lax.broadcasted_iota(jnp.int32, (256, 256), 0)
    place = (m // 16) * 8 + m % 8 + 128 * ((m // 8) % 2)

    for i in range(2048 // ROWS):
        part = pl.ds(i * ROWS, ROWS)
        acc_ref[...] = jnp.dot(single_ref[part, :], phi_ref[...], preferred_element_type=F32) + jnp.dot(
            double_ref[part, :], w_ref[...], preferred_element_type=F32
        )

        def add_near(k, carry, i=i):
            @pl.when((k < count_ref[0]) & (rows_ref[k] // (ROWS // 128) == i))
            def _():
                row = pl.multiple_of((rows_ref[k] % (ROWS // 128)) * 128, 128)
                col = pl.multiple_of(cols_ref[k] * 128, 128)
                acc_ref[pl.ds(row, 128), :] += jnp.dot(
                    near_ref[k], phi_ref[pl.ds(col, 128), :], preferred_element_type=F32
                )

            return carry

        lax.fori_loop(0, 8, add_near, 0)
        total = acc_ref[...].astype(BF)
        if first:
            for p in range(ROWS // 256):
                pair = i * (ROWS // 256) + p
                select = (place == keys[0][pair]).astype(F32).astype(BF)
                packed = jnp.dot(select, total[p * 256 : p * 256 + 256], preferred_element_type=F32).astype(BF)
                out_ref[:, pair * 16 : pair * 16 + 16, :] = packed.reshape(16, 16, WAVES)
        else:
            owners = ROWS // 128
            out_ref[i * owners : (i + 1) * owners, 0:128, :] = total.reshape(owners, 128, WAVES)
    out_ref[:, 128:136, :] = extra_ref[...]


def boundary(order, near, chunks, matrices, extra, *keys):
    near_blocks, near_rows, near_cols, near_count = near
    first = len(keys) > 0
    vmem = pl.BlockSpec(memory_space=pltpu.VMEM)
    return pl.pallas_call(
        lambda *refs: boundary_kernel(first, *refs),
        in_specs=[pl.BlockSpec(memory_space=pltpu.SMEM)] * 4 + [vmem] * (12 + len(keys)),
        out_specs=vmem,
        out_shape=jax.ShapeDtypeStruct((16, 136, WAVES), BF),
        scratch_shapes=[
            pltpu.VMEM((1024, WAVES), BF),
            pltpu.VMEM((1024, WAVES), BF),
            pltpu.VMEM((ROWS, WAVES), F32),
        ],
        compiler_params=pltpu.CompilerParams(vmem_limit_bytes=LIMIT << 20),
        name="boundary_first" if first else "boundary_second",
    )(order, near_rows, near_cols, near_count, *chunks, *matrices, near_blocks, extra, *keys)


def faces_kernel(side_ref, low_x, high_x, low_y, high_y, sib, far, even, odd):
    row_even = side_ref[0] == 0
    col_even = side_ref[1] == 0
    sib[...] = jnp.where(row_even, high_x[...], low_x[...]).astype(BF)
    far[...] = jnp.where(row_even, low_x[...], high_x[...]).astype(BF)
    even[...] = jnp.where(col_even, high_y[...], low_y[...]).astype(BF)
    odd[...] = jnp.where(col_even, low_y[...], high_y[...]).astype(BF)


def faces_of(side, field):
    across = lambda at: pl.BlockSpec((3, None, 8, 8, WAVES), lambda i: (0, at, 0, 0, 0))
    along = lambda at: pl.BlockSpec((3, 8, None, 8, WAVES), lambda i: (0, 0, at, 0, 0))
    out = pl.BlockSpec((3, 8, 8, WAVES), lambda i: (0, 0, 0, 0))
    return pl.pallas_call(
        faces_kernel,
        grid=(1,),
        in_specs=[pl.BlockSpec(memory_space=pltpu.SMEM), across(0), across(7), along(0), along(7)],
        out_specs=[out] * 4,
        out_shape=[jax.ShapeDtypeStruct((3, 8, 8, WAVES), BF)] * 4,
        compiler_params=pltpu.CompilerParams(vmem_limit_bytes=8 << 20),
        name="faces",
    )(side, *[in_hbm(field)] * 4)


def middle_kernel(got_ref, chunk_ref, out_ref):
    total = got_ref[0, 0:128].astype(F32)
    for k in range(1, 16):
        total = total + got_ref[k, 0:128].astype(F32)
    out_ref[0] = (total - 0.5 * chunk_ref[...].astype(F32)).astype(BF)
    out_ref[1] = got_ref[:, 128:136, :].reshape(128, LANES)


def middle(got, chunk):
    return pl.pallas_call(
        middle_kernel,
        grid=(WAVES // LANES,),
        in_specs=[
            pl.BlockSpec((16, 136, LANES), lambda i: (0, 0, i)),
            pl.BlockSpec((None, 128, LANES), lambda i: (1, 0, i)),
        ],
        out_specs=pl.BlockSpec((2, 128, LANES), lambda i: (0, 0, i)),
        out_shape=jax.ShapeDtypeStruct((2, 128, WAVES), BF),
        compiler_params=pltpu.CompilerParams(vmem_limit_bytes=8 << 20),
        name="middle",
    )(got, chunk)


def last_kernel(got_ref, w_ref, route_ref, comp_ref, _, flux_ref, field_ref, mid_ref, new_ref, sems):
    picker = (lax.broadcasted_iota(jnp.int32, (128, 128), 1) == route_ref[...]).astype(F32).astype(BF)
    mid_ref[...] = jnp.dot(picker, got_ref[:, 128:136, :].reshape(128, WAVES), preferred_element_type=F32)
    depth = lax.broadcasted_iota(jnp.int32, (8, WAVES), 0)
    copies = []
    for half in range(2):

        def step(x, carry):
            for y in range(8):
                low = mid_ref[pl.ds(x * 8 + y, 1), :]
                high = mid_ref[pl.ds(64 + x * 8 + y, 1), :]
                new_ref[x, y] = comp_ref[x, y] - jnp.where(depth == 0, low, jnp.where(depth == 7, high, 0.0))
            return carry

        lax.fori_loop(half * 4, half * 4 + 4, step, 0)
        part = pl.ds(half * 4, 4)
        copy = pltpu.make_async_copy(new_ref.at[part], field_ref.at[2, part], sems.at[half])
        copy.start()
        copies.append(copy)
    for row in range(0, 128, 32):
        part = slice(row, row + 32)
        total = got_ref[0, part].astype(F32)
        for k in range(1, 16):
            total = total + got_ref[k, part].astype(F32)
        flux_ref[part, :] = total - 0.5 * w_ref[part, :]
    for copy in copies:
        copy.wait()


def last(got, trace, route_column, comp, field):
    vmem = pl.BlockSpec(memory_space=pltpu.VMEM)
    hbm = pl.BlockSpec(memory_space=pltpu.HBM)
    return pl.pallas_call(
        last_kernel,
        in_specs=[vmem, vmem, vmem, vmem, hbm],
        out_specs=[vmem, hbm],
        out_shape=[jax.ShapeDtypeStruct((128, WAVES), F32), jax.ShapeDtypeStruct(field.shape, F32)],
        scratch_shapes=[
            pltpu.VMEM((128, WAVES), F32),
            pltpu.VMEM((8, 8, 8, WAVES), F32),
            pltpu.SemaphoreType.DMA((2,)),
        ],
        input_output_aliases={4: 1},
        compiler_params=pltpu.CompilerParams(vmem_limit_bytes=8 << 20),
        name="last",
    )(got, trace, route_column, comp, in_hbm(field))


def shifted(count, by):
    return [(i, (i + by) % count) for i in range(count)]


def in_hbm(array):
    return pltpu.with_memory_space_constraint(array, pltpu.HBM)


def swapped(count, bits):
    return [(i, i ^ bits) for i in range(count)]


def across_rows(chunk):
    mine = [chunk] + [lax.ppermute(chunk, "row", swapped(8, k)) for k in (4, 2, 6)]
    beside = [lax.ppermute(one, "row", swapped(8, 1)) for one in mine]
    order = lax.axis_index("row") ^ jnp.array([0, 4, 2, 6, 1, 5, 3, 7], jnp.int32)
    return mine + beside, order


def swap_faces(sib, far, even, odd):
    across = lambda count: [pair for i in range(1, count - 1, 2) for pair in ((i, i + 1), (i + 1, i))]
    return (
        lax.ppermute(sib, "row", swapped(8, 1)),
        lax.ppermute(far, "row", across(8)),
        lax.ppermute(even, "col", swapped(16, 1)),
        lax.ppermute(odd, "col", across(16)),
    )


def after(value, *others):
    return lax.optimization_barrier((value, *others))[0]


def local(
    displacement,
    flux,
    stiffness,
    mixing,
    single_layer,
    double_layer,
    near_blocks,
    near_rows,
    near_cols,
    near_counts,
    routes,
):
    near = (near_blocks.reshape(8, 128, 128), near_rows.reshape(8), near_cols.reshape(8), near_counts.reshape(1))
    route_row = routes.reshape(1, 128)
    side = jnp.stack([lax.axis_index("row") % 2, lax.axis_index("col") % 2]).astype(jnp.int32)
    stiff = stiffness[..., None]

    packed = pack(flux, displacement, route_row)
    got = lax.all_to_all(packed.reshape(16, 8, 2 * WAVES + 128), "col", 0, 0, tiled=True)
    halos = swap_faces(*faces_of(side, displacement))
    field, trace, outgoing, *faces = stencil(side, displacement, halos, stiff, mixing, flux, route_row)
    got = after(got, outgoing)
    chunk = jnp.stack(
        [got[:, :, :WAVES].reshape(128, WAVES), got[:, :, WAVES : 2 * WAVES].reshape(128, WAVES)], 0
    )
    keys = got[:, 0, 2 * WAVES :].astype(jnp.int32).reshape(8, 2, 128)
    keys = (keys + jnp.array([0, 128], jnp.int32)[None, :, None]).reshape(8, 1, 256)

    matrices = stage(after(side, chunk), single_layer, double_layer)
    chunks, order = across_rows(chunk)
    sums = boundary(order, near, chunks, matrices, outgoing.reshape(16, 8, WAVES), keys)
    got = lax.all_to_all(sums, "col", 0, 0, tiled=True)
    halos = swap_faces(*after(faces, sums))
    chunk = middle(after(got, halos), chunk)
    matrices = stage(after(side, chunk), single_layer, double_layer)

    chunks, order = across_rows(chunk)
    sums = boundary(order, near, chunks, matrices, chunk[0].reshape(16, 8, WAVES))
    got = lax.all_to_all(sums, "col", 0, 0, tiled=True)
    field, comp = stencil(side, field, after(halos, sums), stiff, mixing)
    new_flux, field = last(after(got, comp), trace, routes.reshape(128, 1), comp, field)
    return (field, new_flux)


def solution(mesh):
    return jax.shard_map(
        local,
        mesh=mesh,
        in_specs=(
            P(None, "row", "col", None, None),
            P(("row", "col"), None),
            P("row", "col", None),
            P(),
            P("row", "col"),
            P("row", "col"),
            P("row", "col", None, None),
            P("row", "col"),
            P("row", "col"),
            P("row", "col"),
            P(("row", "col")),
        ),
        out_specs=(P(None, "row", "col", None, None), P(("row", "col"), None)),
        check_vma=False,
    )
```

```python
import jax
import jax.numpy as jnp
from jax import lax
from jax.experimental import pallas as pl
from jax.experimental.pallas import tpu as pltpu
from jax.sharding import PartitionSpec as P

BF = jnp.bfloat16
F32 = jnp.float32
WAVES = 384
LANES = 128
ROWS = 512
LIMIT = 12


def onehot(keys, count):
    rows = lax.broadcasted_iota(jnp.int32, (count, keys.shape[1]), 0)
    return (rows == keys).astype(F32).astype(BF)


def pack_kernel(flux_ref, comp_ref, route_ref, out_ref, trace_ref):
    by_panel = onehot(route_ref[...], 128)
    out_ref[:, 0:WAVES] = jnp.dot(by_panel, flux_ref[...].astype(BF), preferred_element_type=F32).astype(BF)

    for x in range(8):
        trace_ref[x * 8 : x * 8 + 8, :] = comp_ref[x, :, 0, :]
        trace_ref[64 + x * 8 : 64 + x * 8 + 8, :] = comp_ref[x, :, 7, :]
    out_ref[:, WAVES : 2 * WAVES] = jnp.dot(
        by_panel, trace_ref[...].astype(BF), preferred_element_type=F32
    ).astype(BF)
    out_ref[:, 2 * WAVES :] = jnp.broadcast_to(route_ref[...].astype(F32), (128, 128)).astype(BF)


def pack(flux, field, route_row):
    return pl.pallas_call(
        pack_kernel,
        grid=(1,),
        in_specs=[
            pl.BlockSpec((128, WAVES), lambda i: (0, 0)),
            pl.BlockSpec((None, 8, 8, 8, WAVES), lambda i: (2, 0, 0, 0, 0)),
            pl.BlockSpec((1, 128), lambda i: (0, 0)),
        ],
        out_specs=pl.BlockSpec((128, 2 * WAVES + 128), lambda i: (0, 0)),
        out_shape=jax.ShapeDtypeStruct((128, 2 * WAVES + 128), BF),
        scratch_shapes=[pltpu.VMEM((128, WAVES), F32)],
        compiler_params=pltpu.CompilerParams(vmem_limit_bytes=8 << 20),
        name="pack",
    )(in_hbm(flux), in_hbm(field), route_row)


def stencil_kernel(first, side_ref, mix_ref, *refs):
    if first:
        u_ref, sib, far, even, odd, st_ref, flux_ref, route_ref, out_ref, w_ref, wp_ref, f_sib, f_far, f_even, f_odd = refs
    else:
        u_ref, sib, far, even, odd, st_ref, out_ref, comp_ref = refs
    row_even = side_ref[0] == 0
    col_even = side_ref[1] == 0

    def low_x(c, y):
        return jnp.where(row_even, far[c, y], sib[c, y]).astype(F32)

    def high_x(c, y):
        return jnp.where(row_even, sib[c, y], far[c, y]).astype(F32)

    def low_y(c, x):
        return jnp.where(col_even, odd[c, x], even[c, x]).astype(F32)

    def high_y(c, x):
        return jnp.where(col_even, even[c, x], odd[c, x]).astype(F32)

    depth = lax.broadcasted_iota(jnp.int32, (8, LANES), 0)
    bottom = depth == 0
    top = depth == 7
    mix = [[mix_ref[i, j] for j in range(3)] for i in range(3)]

    def plane(x, below, above):
        for y in range(8):
            cell = [u_ref[c, x, y] for c in range(3)]
            stiff = jnp.broadcast_to(st_ref[x, y], (8, LANES))
            for c in range(3):
                u = cell[c]
                total = below(c, y) + above(c, y)
                total = total + (u_ref[c, x, y - 1] if y > 0 else low_y(c, x))
                total = total + (u_ref[c, x, y + 1] if y < 7 else high_y(c, x))
                total = total + jnp.where(bottom, 0.0, pltpu.roll(u, 1, 0))
                total = total + jnp.where(top, 0.0, pltpu.roll(u, 7, 0))
                mixed = mix[c][0] * cell[0] + mix[c][1] * cell[1] + mix[c][2] * cell[2]
                value = stiff * (u - total * (1.0 / 6.0)) + mixed
                if first and c == 2:
                    low = flux_ref[pl.ds(x * 8 + y, 1), :]
                    high = flux_ref[pl.ds(64 + x * 8 + y, 1), :]
                    value = value - jnp.where(bottom, low, jnp.where(top, high, 0.0))
                    w_ref[pl.ds(x * 8 + y, 1), :] = value[0:1]
                    w_ref[pl.ds(64 + x * 8 + y, 1), :] = value[7:8]
                if first or c < 2:
                    out_ref[c, x, y] = value
                else:
                    comp_ref[x, y] = value

    plane(0, low_x, lambda c, y: u_ref[c, 1, y])

    def step(x, carry):
        plane(x, lambda c, y: u_ref[c, x - 1, y], lambda c, y: u_ref[c, x + 1, y])
        return carry

    lax.fori_loop(1, 7, step, 0)
    plane(7, lambda c, y: u_ref[c, 6, y], high_x)
    if first:
        f_sib[...] = jnp.where(row_even, out_ref[:, 7], out_ref[:, 0]).astype(BF)
        f_far[...] = jnp.where(row_even, out_ref[:, 0], out_ref[:, 7]).astype(BF)
        f_even[...] = jnp.where(col_even, out_ref[:, :, 7], out_ref[:, :, 0]).astype(BF)
        f_odd[...] = jnp.where(col_even, out_ref[:, :, 0], out_ref[:, :, 7]).astype(BF)
        wp_ref[...] = jnp.dot(onehot(route_ref[...], 128), w_ref[...].astype(BF), preferred_element_type=F32).astype(BF)


def stencil(side, field, halos, stiffness, mixing, flux=None, route_row=None):
    first = flux is not None
    whole = pl.BlockSpec((3, 8, 8, 8, LANES), lambda i: (0, 0, 0, 0, i))
    face = pl.BlockSpec((3, 8, 8, LANES), lambda i: (0, 0, 0, i))
    panel = pl.BlockSpec((128, LANES), lambda i: (0, i))
    in_specs = [pl.BlockSpec(memory_space=pltpu.SMEM)] * 2 + [whole, face, face, face, face,
                pl.BlockSpec((8, 8, 8, 1), lambda i: (0, 0, 0, 0))]
    args = [side, mixing, in_hbm(field), *halos, stiffness]
    out_specs = [whole if first else pl.BlockSpec((2, 8, 8, 8, LANES), lambda i: (0, 0, 0, 0, i))]
    out_shape = [pltpu.HBM(field.shape, F32)]
    if not first:
        out_specs += [pl.BlockSpec((8, 8, 8, LANES), lambda i: (0, 0, 0, i))]
        out_shape += [jax.ShapeDtypeStruct(field.shape[1:], F32)]
    if first:
        in_specs += [panel, pl.BlockSpec((1, 128), lambda i: (0, 0))]
        args += [flux, route_row]
        out_specs += [panel, panel, face, face, face, face]
        out_shape += [jax.ShapeDtypeStruct((128, WAVES), F32), jax.ShapeDtypeStruct((128, WAVES), BF)]
        out_shape += [jax.ShapeDtypeStruct((3, 8, 8, WAVES), BF)] * 4
    return pl.pallas_call(
        lambda *refs: stencil_kernel(first, *refs),
        grid=(WAVES // LANES,),
        in_specs=in_specs,
        out_specs=out_specs,
        out_shape=out_shape,
        compiler_params=pltpu.CompilerParams(vmem_limit_bytes=8 << 20),
        name="stencil_first" if first else "stencil_second",
    )(*args)


def stage_kernel(side_ref, single_hbm, double_hbm, single_ref, double_ref, sems):
    copies = [
        pltpu.make_async_copy(single_hbm, single_ref, sems.at[0]),
        pltpu.make_async_copy(double_hbm, double_ref, sems.at[1]),
    ]
    for copy in copies:
        copy.start()
    for copy in copies:
        copy.wait()


def stage(side, single_layer, double_layer):
    hbm = pl.BlockSpec(memory_space=pltpu.HBM)
    return pl.pallas_call(
        stage_kernel,
        in_specs=[pl.BlockSpec(memory_space=pltpu.SMEM), hbm, hbm],
        out_specs=[pl.BlockSpec(memory_space=pltpu.VMEM)] * 2,
        out_shape=[pltpu.VMEM((2048, 1024), BF)] * 2,
        scratch_shapes=[pltpu.SemaphoreType.DMA((2,))],
        compiler_params=pltpu.CompilerParams(vmem_limit_bytes=10 << 20),
        name="stage",
    )(side, in_hbm(single_layer), in_hbm(double_layer))


def boundary_kernel(first, order_ref, rows_ref, cols_ref, count_ref, *refs):
    chunks = refs[:8]
    single_ref, double_ref, near_ref = refs[8:11]
    extra_ref, *keys, out_ref, phi_ref, w_ref, acc_ref = refs[11:]
    for k in range(8):
        at = pl.multiple_of(order_ref[k] * 128, 128)
        phi_ref[pl.ds(at, 128), :] = chunks[k][0]
        w_ref[pl.ds(at, 128), :] = chunks[k][1]
    m = lax.broadcasted_iota(jnp.int32, (256, 256), 0)
    place = (m // 16) * 8 + m % 8 + 128 * ((m // 8) % 2)

    for i in range(2048 // ROWS):
        part = pl.ds(i * ROWS, ROWS)
        acc_ref[part, :] = jnp.dot(single_ref[part, :], phi_ref[...], preferred_element_type=F32) + jnp.dot(
            double_ref[part, :], w_ref[...], preferred_element_type=F32
        )

    def add_near(k, carry):
        row = pl.multiple_of(rows_ref[k] * 128, 128)
        col = pl.multiple_of(cols_ref[k] * 128, 128)
        acc_ref[pl.ds(row, 128), :] += jnp.dot(
            near_ref[k], phi_ref[pl.ds(col, 128), :], preferred_element_type=F32
        )
        return carry

    lax.fori_loop(0, jnp.minimum(count_ref[0], 8), add_near, 0)
    if first:
        for pair in range(8):
            total = acc_ref[pair * 256 : pair * 256 + 256, :].astype(BF)
            select = (place == keys[0][pair]).astype(F32).astype(BF)
            packed = jnp.dot(select, total, preferred_element_type=F32).astype(BF)
            out_ref[:, pair * 16 : pair * 16 + 16, :] = packed.reshape(16, 16, WAVES)
    else:
        out_ref[:, 0:128, :] = acc_ref[...].astype(BF).reshape(16, 128, WAVES)
    out_ref[:, 128:136, :] = extra_ref[...]


def boundary(order, near, chunks, matrices, extra, *keys):
    near_blocks, near_rows, near_cols, near_count = near
    first = len(keys) > 0
    vmem = pl.BlockSpec(memory_space=pltpu.VMEM)
    return pl.pallas_call(
        lambda *refs: boundary_kernel(first, *refs),
        in_specs=[pl.BlockSpec(memory_space=pltpu.SMEM)] * 4 + [vmem] * (12 + len(keys)),
        out_specs=vmem,
        out_shape=jax.ShapeDtypeStruct((16, 136, WAVES), BF),
        scratch_shapes=[
            pltpu.VMEM((1024, WAVES), BF),
            pltpu.VMEM((1024, WAVES), BF),
            pltpu.VMEM((2048, WAVES), F32),
        ],
        compiler_params=pltpu.CompilerParams(vmem_limit_bytes=LIMIT << 20),
        name="boundary_first" if first else "boundary_second",
    )(order, near_rows, near_cols, near_count, *chunks, *matrices, near_blocks, extra, *keys)


def faces_kernel(side_ref, low_x, high_x, low_y, high_y, sib, far, even, odd):
    row_even = side_ref[0] == 0
    col_even = side_ref[1] == 0
    sib[...] = jnp.where(row_even, high_x[...], low_x[...]).astype(BF)
    far[...] = jnp.where(row_even, low_x[...], high_x[...]).astype(BF)
    even[...] = jnp.where(col_even, high_y[...], low_y[...]).astype(BF)
    odd[...] = jnp.where(col_even, low_y[...], high_y[...]).astype(BF)


def faces_of(side, field):
    across = lambda at: pl.BlockSpec((3, None, 8, 8, WAVES), lambda i: (0, at, 0, 0, 0))
    along = lambda at: pl.BlockSpec((3, 8, None, 8, WAVES), lambda i: (0, 0, at, 0, 0))
    out = pl.BlockSpec((3, 8, 8, WAVES), lambda i: (0, 0, 0, 0))
    return pl.pallas_call(
        faces_kernel,
        grid=(1,),
        in_specs=[pl.BlockSpec(memory_space=pltpu.SMEM), across(0), across(7), along(0), along(7)],
        out_specs=[out] * 4,
        out_shape=[jax.ShapeDtypeStruct((3, 8, 8, WAVES), BF)] * 4,
        compiler_params=pltpu.CompilerParams(vmem_limit_bytes=8 << 20),
        name="faces",
    )(side, *[in_hbm(field)] * 4)


def middle_kernel(got_ref, chunk_ref, out_ref):
    total = got_ref[0, 0:128].astype(F32)
    for k in range(1, 16):
        total = total + got_ref[k, 0:128].astype(F32)
    out_ref[0] = (total - 0.5 * chunk_ref[...].astype(F32)).astype(BF)
    out_ref[1] = got_ref[:, 128:136, :].reshape(128, LANES)


def middle(got, chunk):
    return pl.pallas_call(
        middle_kernel,
        grid=(WAVES // LANES,),
        in_specs=[
            pl.BlockSpec((16, 136, LANES), lambda i: (0, 0, i)),
            pl.BlockSpec((None, 128, LANES), lambda i: (1, 0, i)),
        ],
        out_specs=pl.BlockSpec((2, 128, LANES), lambda i: (0, 0, i)),
        out_shape=jax.ShapeDtypeStruct((2, 128, WAVES), BF),
        compiler_params=pltpu.CompilerParams(vmem_limit_bytes=8 << 20),
        name="middle",
    )(got, chunk)


def last_kernel(got_ref, w_ref, route_ref, comp_ref, _, flux_ref, field_ref, mid_ref, new_ref, sems):
    picker = (lax.broadcasted_iota(jnp.int32, (128, 128), 1) == route_ref[...]).astype(F32).astype(BF)
    mid_ref[...] = jnp.dot(picker, got_ref[:, 128:136, :].reshape(128, WAVES), preferred_element_type=F32)
    depth = lax.broadcasted_iota(jnp.int32, (8, WAVES), 0)
    copies = []
    for half in range(2):

        def step(x, carry):
            for y in range(8):
                low = mid_ref[pl.ds(x * 8 + y, 1), :]
                high = mid_ref[pl.ds(64 + x * 8 + y, 1), :]
                new_ref[x, y] = comp_ref[x, y] - jnp.where(depth == 0, low, jnp.where(depth == 7, high, 0.0))
            return carry

        lax.fori_loop(half * 4, half * 4 + 4, step, 0)
        part = pl.ds(half * 4, 4)
        copy = pltpu.make_async_copy(new_ref.at[part], field_ref.at[2, part], sems.at[half])
        copy.start()
        copies.append(copy)
    for row in range(0, 128, 32):
        part = slice(row, row + 32)
        total = got_ref[0, part].astype(F32)
        for k in range(1, 16):
            total = total + got_ref[k, part].astype(F32)
        flux_ref[part, :] = total - 0.5 * w_ref[part, :]
    for copy in copies:
        copy.wait()


def last(got, trace, route_column, comp, field):
    vmem = pl.BlockSpec(memory_space=pltpu.VMEM)
    hbm = pl.BlockSpec(memory_space=pltpu.HBM)
    return pl.pallas_call(
        last_kernel,
        in_specs=[vmem, vmem, vmem, vmem, hbm],
        out_specs=[vmem, hbm],
        out_shape=[jax.ShapeDtypeStruct((128, WAVES), F32), jax.ShapeDtypeStruct(field.shape, F32)],
        scratch_shapes=[
            pltpu.VMEM((128, WAVES), F32),
            pltpu.VMEM((8, 8, 8, WAVES), F32),
            pltpu.SemaphoreType.DMA((2,)),
        ],
        input_output_aliases={4: 1},
        compiler_params=pltpu.CompilerParams(vmem_limit_bytes=8 << 20),
        name="last",
    )(got, trace, route_column, comp, in_hbm(field))


def shifted(count, by):
    return [(i, (i + by) % count) for i in range(count)]


def in_hbm(array):
    return pltpu.with_memory_space_constraint(array, pltpu.HBM)


def swapped(count, bits):
    return [(i, i ^ bits) for i in range(count)]


def across_rows(chunk):
    mine = [chunk] + [lax.ppermute(chunk, "row", swapped(8, k)) for k in (4, 2, 6)]
    beside = [lax.ppermute(one, "row", swapped(8, 1)) for one in mine]
    order = lax.axis_index("row") ^ jnp.array([0, 4, 2, 6, 1, 5, 3, 7], jnp.int32)
    return mine + beside, order


def swap_faces(sib, far, even, odd):
    across = lambda count: [pair for i in range(1, count - 1, 2) for pair in ((i, i + 1), (i + 1, i))]
    return (
        lax.ppermute(sib, "row", swapped(8, 1)),
        lax.ppermute(far, "row", across(8)),
        lax.ppermute(even, "col", swapped(16, 1)),
        lax.ppermute(odd, "col", across(16)),
    )


def after(value, *others):
    return lax.optimization_barrier((value, *others))[0]


def local(
    displacement,
    flux,
    stiffness,
    mixing,
    single_layer,
    double_layer,
    near_blocks,
    near_rows,
    near_cols,
    near_counts,
    routes,
):
    near = (near_blocks.reshape(8, 128, 128), near_rows.reshape(8), near_cols.reshape(8), near_counts.reshape(1))
    route_row = routes.reshape(1, 128)
    side = jnp.stack([lax.axis_index("row") % 2, lax.axis_index("col") % 2]).astype(jnp.int32)
    stiff = stiffness[..., None]

    packed = pack(flux, displacement, route_row)
    got = lax.all_to_all(packed.reshape(16, 8, 2 * WAVES + 128), "col", 0, 0, tiled=True)
    halos = swap_faces(*faces_of(side, displacement))
    field, trace, outgoing, *faces = stencil(side, displacement, halos, stiff, mixing, flux, route_row)
    got = after(got, outgoing)
    chunk = jnp.stack(
        [got[:, :, :WAVES].reshape(128, WAVES), got[:, :, WAVES : 2 * WAVES].reshape(128, WAVES)], 0
    )
    keys = got[:, 0, 2 * WAVES :].astype(jnp.int32).reshape(8, 2, 128)
    keys = (keys + jnp.array([0, 128], jnp.int32)[None, :, None]).reshape(8, 1, 256)

    matrices = stage(after(side, chunk), single_layer, double_layer)
    chunks, order = across_rows(chunk)
    sums = boundary(order, near, chunks, matrices, outgoing.reshape(16, 8, WAVES), keys)
    got = lax.all_to_all(sums, "col", 0, 0, tiled=True)
    halos = swap_faces(*after(faces, sums))
    chunk = middle(after(got, halos), chunk)
    matrices = stage(after(side, chunk), single_layer, double_layer)

    chunks, order = across_rows(chunk)
    sums = boundary(order, near, chunks, matrices, chunk[0].reshape(16, 8, WAVES))
    got = lax.all_to_all(sums, "col", 0, 0, tiled=True)
    field, comp = stencil(side, field, after(halos, sums), stiff, mixing)
    new_flux, field = last(after(got, comp), trace, routes.reshape(128, 1), comp, field)
    return (field, new_flux)


def solution(mesh):
    return jax.shard_map(
        local,
        mesh=mesh,
        in_specs=(
            P(None, "row", "col", None, None),
            P(("row", "col"), None),
            P("row", "col", None),
            P(),
            P("row", "col"),
            P("row", "col"),
            P("row", "col", None, None),
            P("row", "col"),
            P("row", "col"),
            P("row", "col"),
            P(("row", "col")),
        ),
        out_specs=(P(None, "row", "col", None, None), P(("row", "col"), None)),
        check_vma=False,
    )
```
